32 devices in a mesh: rep: 8 (over z, x), mp: 4 (over y, core).
Axes of the slice: x: 2, y: 2, z: 4, core: 2. Of those that a mesh axis runs over, the one named last changes fastest.
Arguments:
- weight: bfloat16 [4096, 4096], P('rep', 'mp'), may hold values from -4 to 4
- tokens: bfloat16 [2048, 4096], P('rep', 'mp'), may hold values from -16 to 16
- cotangent: bfloat16 [2048, 4096], P('rep', 'mp'), may hold values from -128 to 128
- next_tokens: bfloat16 [2048, 4096], P('rep'), may hold values from -6 to 6
Outputs:
- new_weight: bfloat16 [4096, 4096], P('rep', 'mp')
- next_query: bfloat16 [2048, 4096], P('rep', 'mp')
The draws below stay inside these ranges and needn't reach their ends.
All inputs are finite; a program needn't handle non-finite values.
Results may differ from the reference program's by a relative error of at most 0.0049.
Values may be sent and summed in bfloat16 or wider, within the bound.
A program may use at most 128 MiB of HBM per device.

```python
import jax
import jax.numpy as jnp

D = 4096
TOK_DEV = 256
GRADIENT_TOKENS = 2048
NEXT = 2048


def shared_weights(key, copies):
    freqs = jax.random.uniform(jax.random.fold_in(key, 1), (copies, 1), minval=0.5, maxval=2.5)
    phases = jax.random.uniform(jax.random.fold_in(key, 2), (copies, 1), minval=0.0, maxval=6.2831853)
    position = (jnp.arange(D).astype(jnp.float32) / D)[None, :]
    waves = jnp.cos(6.2831853 * freqs * position + phases)
    return jnp.repeat(waves, TOK_DEV, axis=0)


def row_weights(key):
    position = jnp.arange(GRADIENT_TOKENS) % TOK_DEV
    base = jnp.where(position < TOK_DEV // 4, 0.3, 1.2).astype(jnp.float32)
    spike_amount = jax.random.bernoulli(jax.random.fold_in(key, 99), 0.03, (GRADIENT_TOKENS,))
    amplify_factor = jnp.where(spike_amount, 3.0, 1.0).astype(jnp.float32)
    return (base * amplify_factor)[:, None]


def draw_tokens(key, part):
    copies = GRADIENT_TOKENS // TOK_DEV
    mixing = shared_weights(jax.random.fold_in(key, 17), copies)
    mixing_strength = row_weights(key)
    shared = jnp.clip(jax.random.normal(jax.random.fold_in(key, 11), (TOK_DEV, D)), -4.0, 4.0)
    owned = jnp.clip(jax.random.normal(jax.random.fold_in(key, 12), (GRADIENT_TOKENS, D)), -4.0, 4.0)
    values = mixing_strength * mixing * jnp.tile(shared, (copies, 1)) + 0.5 * owned
    return jnp.clip(values, -16.0, 16.0).astype(jnp.bfloat16)


def draw_cotangent(key, part):
    copies = GRADIENT_TOKENS // TOK_DEV
    mixing = shared_weights(jax.random.fold_in(key, 27), copies)
    mixing_strength = row_weights(key)
    owner_replica = (jnp.arange(GRADIENT_TOKENS) // TOK_DEV).astype(jnp.float32)
    replica_scale = (1.0 + 2.0 * owner_replica / max(copies - 1, 1))[:, None]
    heavy = jax.random.bernoulli(jax.random.fold_in(key, 31), 0.01, (1, D))
    shared = jnp.clip(jax.random.normal(jax.random.fold_in(key, 21), (TOK_DEV, D)), -4.0, 4.0)
    owned = jnp.clip(jax.random.normal(jax.random.fold_in(key, 22), (GRADIENT_TOKENS, D)), -4.0, 4.0)
    drawn_scale = (1.0 + 2.0 * jnp.arange(D).astype(jnp.float32) / (D - 1))[None, :]
    column_scale = jnp.where(heavy, 15.0, drawn_scale)
    values = (mixing_strength * mixing * jnp.tile(shared, (copies, 1)) + 0.5 * owned) * replica_scale * column_scale
    return jnp.clip(values, -128.0, 128.0).astype(jnp.bfloat16)


def levels(key, shape, shards, least, top_value):
    level = 1.0
    for axis_at, blocks in shards:
        draws = jax.random.uniform(jax.random.fold_in(jax.random.fold_in(key, 6), axis_at), (blocks,), jnp.float32, least / len(shards), top_value / len(shards))
        level = level * jnp.repeat(jnp.exp(draws), shape[axis_at] // blocks).reshape((-1,) + (1,) * (len(shape) - 1 - axis_at))
    return level


def gaussian(stream_key, dims, deviation, limit, shards=(), held_as=jnp.bfloat16):
    loudness = levels(stream_key, dims, shards, -0.22, 0.18) if shards else 1.0
    result = jax.random.normal(stream_key, dims, jnp.float32) * deviation * loudness
    return jnp.minimum(jnp.maximum(result, -limit), limit).astype(held_as)


def setup_inputs(seed: int = 0) -> dict:
    keys = jax.random.split(jax.random.key(seed), 5)
    weight = gaussian(keys[0], (D, D), 1.0, 4.0, ((0, 8), (1, 4)))
    tokens = draw_tokens(jax.random.fold_in(keys[4], 71), 0)
    cotangent = draw_cotangent(jax.random.fold_in(keys[4], 71), 0)
    next_tokens = gaussian(keys[3], (NEXT, D), 1.0, 6.0, ((0, 8),))
    return dict(weight=weight, tokens=tokens, cotangent=cotangent, next_tokens=next_tokens)


learning_rate = 0.002
eps = 1e-06

def combine(first, second):
    cross_dot = jnp.sum(first * second)
    first_sq = jnp.sum(first * first)
    second_sq = jnp.sum(second * second)
    return (1.0 - cross_dot / (2.0 * first_sq + eps)) * first + (1.0 - cross_dot / (2.0 * second_sq + eps)) * second

def reference(weight, tokens, cotangent, next_tokens):
    replicas = GRADIENT_TOKENS // TOK_DEV

    def leaf_grad(index):
        token_rows = tokens[index * TOK_DEV:(index + 1) * TOK_DEV]
        grad_rows = cotangent[index * TOK_DEV:(index + 1) * TOK_DEV]
        return jnp.dot(token_rows.T, grad_rows, preferred_element_type=jnp.float32)

    def node(index, stride):
        if stride == replicas:
            return leaf_grad(index)
        return combine(node(index, 2 * stride), node(index + stride, 2 * stride))
    update = node(0, 1)
    new_weight = (weight.astype(jnp.float32) - learning_rate * update).astype(jnp.bfloat16)
    product = jnp.dot(next_tokens, new_weight, preferred_element_type=jnp.float32)
    next_query = (product * D ** (-0.5)).astype(jnp.bfloat16)
    return (new_weight, next_query)
```

```python
import functools

import jax
import jax.numpy as jnp
from jax import lax
from jax.experimental import pallas as pl
from jax.experimental.pallas import tpu as pltpu
from jax.sharding import PartitionSpec as P

learning_rate = 0.002
eps = 1e-06
F32 = jnp.float32
BF16 = jnp.bfloat16
MESH = pl.DeviceIdType.MESH
LANES = 128


def x_size(replicas):
    x = 1
    while 2 * (2 * x) ** 2 <= replicas and replicas % (2 * x) == 0:
        x *= 2
    return x


def aligned(start, size):
    return pl.ds(pl.multiple_of(start * size, size), size)


def kernel(
    sizes,
    w_hbm,
    t_hbm,
    c_hbm,
    n_hbm,
    wo_hbm,
    q_hbm,
    cbuf,
    t1buf,
    tfull,
    ttr,
    nbuf,
    grads,
    gloc,
    gmp,
    grep,
    wown,
    wbuf,
    part,
    rsend,
    rrecv,
    qbuf,
    local_sem,
    c_own,
    c_fwd,
    c_xs,
    c_rs,
    t1_s,
    t1_r,
    t2_s,
    t2_r,
    t3_s,
    t3_r,
    n2_s,
    n2_r,
    n3_s,
    n3_r,
    gm_s,
    gm_r,
    gr_s,
    gr_r,
    w_s,
    w_r,
    rs_s,
    rs_r,
):
    Z, X, M, width = sizes
    R = Z * X
    _, tok, cols = cbuf.shape
    rows = tfull.shape[2]
    feats = X * rows
    per = cols // rows
    tq = tok // M
    ntok = nbuf.shape[1]
    nq = ntok // M
    blocks = cols // width
    group = min(8, R)
    grows = gloc.shape[0]

    me = lax.axis_index("rep")
    m = lax.axis_index("mp")
    z = me // X
    x = lax.rem(me, X)

    def nearest(j):
        found = jnp.int32(0)
        for a in range(Z):
            order = sorted(range(Z), key=lambda b: (abs(b - a), b))
            for i in range(Z):
                found = found + jnp.where((z == a) & (j == i), order[i], 0)
        return found

    def remote(src, dst, send, recv, r, mm):
        return pltpu.make_async_remote_copy(
            src_ref=src,
            dst_ref=dst,
            send_sem=send,
            recv_sem=recv,
            device_id=(r, mm),
            device_id_type=MESH,
        )

    def other_x(o):
        return lax.rem(x + o, X)

    def other_m(o):
        return lax.rem(m + o, M)

    def other_r(o):
        return lax.rem(me + o, R)

    def at(zz, xx):
        return zz * X + xx

    def own_copies():
        return [
            pltpu.make_async_copy(c_hbm, cbuf.at[me], local_sem.at[0]),
            pltpu.make_async_copy(t_hbm.at[aligned(m, tq), :], t1buf.at[m], local_sem.at[1]),
            pltpu.make_async_copy(n_hbm.at[:, aligned(z, feats)], nbuf.at[z], local_sem.at[2]),
            pltpu.make_async_copy(w_hbm, wown, local_sem.at[3]),
        ]

    for copy in own_copies():
        copy.start()

    barrier = pltpu.get_barrier_semaphore()
    for o in range(1, M):
        pl.semaphore_signal(barrier, inc=1, device_id=(me, other_m(o)), device_id_type=MESH)
    for o in range(1, R):
        pl.semaphore_signal(barrier, inc=1, device_id=(other_r(o), m), device_id_type=MESH)
    pl.semaphore_wait(barrier, M + R - 2)

    def t1(o):
        mm = other_m(o)
        return remote(t_hbm.at[aligned(mm, tq), :], t1buf.at[m], t1_s.at[o], t1_r.at[o], me, mm)

    for o in range(1, M):
        t1(o).start()

    def c_up():
        return remote(c_hbm, cbuf.at[me], c_own.at[0], c_rs.at[me], at(z + 1, x), m)

    def c_down():
        return remote(c_hbm, cbuf.at[me], c_own.at[1], c_rs.at[me], at(z - 1, x), m)

    def c_across(j, o):
        r = at(nearest(j), x)
        return remote(cbuf.at[r], cbuf.at[r], c_xs.at[j, o], c_rs.at[r], at(z, other_x(o)), m)

    def c_forward(j):
        zz = nearest(j)
        r = at(zz, x)
        to = jnp.where(zz < z, z + 1, z - 1)
        return (
            (to >= 0) & (to < Z),
            lambda: remote(cbuf.at[r], cbuf.at[r], c_fwd.at[j], c_rs.at[r], at(to, x), m),
        )

    pl.when(z < Z - 1)(lambda: c_up().start())
    pl.when(z > 0)(lambda: c_down().start())
    own = own_copies()
    own[0].wait()
    for o in range(1, X):
        c_across(0, o).start()

    def zero(i, carry):
        for r in range(R):
            grads[r, aligned(i, 8), :] = jnp.zeros((8, cols), F32)
        return carry

    lax.fori_loop(0, rows // 8, zero, 0)
    gloc[...] = jnp.zeros_like(gloc)

    own[1].wait()
    for o in range(1, M):
        t1(o).wait_recv()

    def t2_src(r):
        return t1buf.at[r // per, :, aligned(lax.rem(r, per), rows)]

    def t2(o):
        r = other_r(o)
        return remote(t2_src(r), tfull.at[me, aligned(m, tq), :], t2_s.at[o], t2_r.at[me], r, m)

    for o in range(1, R):
        t2(o).start()
    mine = pltpu.make_async_copy(t2_src(me), tfull.at[me, aligned(m, tq), :], local_sem.at[4])
    mine.start()
    mine.wait()

    def t3(r, o):
        piece = tfull.at[r, aligned(m, tq), :]
        return remote(piece, piece, t3_s.at[r], t3_r.at[r], me, other_m(o))

    def t3_start(r):
        for o in range(1, M):
            t3(r, o).start()

    def wait_all(buffer, sem):
        pltpu.make_async_copy(buffer, buffer, sem).wait()

    def t3_wait(r, sem):
        wait_all(tfull.at[r, pl.ds(0, (M - 1) * tq), :], sem.at[r])

    def t2_wait(r):
        piece = tfull.at[r, aligned(m, tq), :]
        pltpu.make_async_copy(piece, piece, t2_r.at[r]).wait()

    t3_start(me)
    for o in range(1, X):
        r = at(z, other_x(o))
        t2_wait(r)
        t3_start(r)

    def n2(o):
        zz = lax.rem(z + o, Z)
        return remote(
            n_hbm.at[aligned(m, nq), aligned(zz, feats)],
            nbuf.at[z, aligned(m, nq), :],
            n2_s.at[o],
            n2_r.at[z],
            at(zz, x),
            m,
        )

    def n3(zz, o):
        piece = nbuf.at[zz, aligned(m, nq), :]
        return remote(piece, piece, n3_s.at[zz], n3_r.at[zz], me, other_m(o))

    def n2_start():
        for o in range(1, Z):
            n2(o).start()

    def n3_start():
        for o in range(1, Z):
            zz = lax.rem(z + o, Z)
            piece = nbuf.at[zz, aligned(m, nq), :]
            pltpu.make_async_copy(piece, piece, n2_r.at[zz]).wait()
            for p in range(1, M):
                n3(zz, p).start()

    def process(r):
        ttr[...] = tfull[r].T
        tile = min(256, cols)

        def grad_tile(i, carry):
            at_cols = aligned(i, tile)
            grads[r, :, at_cols] = jnp.dot(
                ttr[...], cbuf[r, :, at_cols], preferred_element_type=F32
            )
            return carry

        lax.fori_loop(0, cols // tile, grad_tile, 0)
        sub = lax.broadcasted_iota(jnp.int32, gloc.shape, 0)
        lane = lax.broadcasted_iota(jnp.int32, gloc.shape, 1)

        def dots(g, carry):
            def row(i, sums):
                new = grads[r, aligned(i, 8), :]
                out = []
                for q in range(group):
                    prod = new * grads[g * group + q, aligned(i, 8), :]
                    total = sums[q]
                    for a in range(cols // LANES):
                        total = total + prod[:, a * LANES : (a + 1) * LANES]
                    out.append(total)
                return tuple(out)

            sums = lax.fori_loop(
                0, rows // 8, row, tuple(jnp.zeros((8, LANES), F32) for _ in range(group))
            )
            gram = gloc[...]
            for q in range(group):
                other = g * group + q
                total = jnp.sum(jnp.sum(sums[q], axis=1, keepdims=True), axis=0, keepdims=True)
                here = ((sub == r) & (lane == other)) | ((sub == other) & (lane == r))
                gram = gram + jnp.where(here, total, 0.0)
            gloc[...] = gram
            return carry

        lax.fori_loop(0, R // group, dots, 0)

    def step(j, carry):
        zz = nearest(j)

        @pl.when((j >= 1) & (j < Z))
        def _():
            r = at(zz, x)
            pltpu.make_async_copy(cbuf.at[r], cbuf.at[r], c_rs.at[r]).wait()
            ok, copy = c_forward(j)
            pl.when(ok)(lambda: copy().start())
            for o in range(1, X):
                c_across(j, o).start()

        @pl.when(j < Z - 1)
        def _():
            ahead = nearest(j + 1)
            for o in range(X):
                r = at(ahead, other_x(o))
                t2_wait(r)
                t3_start(r)

        pl.when(j == Z - 2)(n2_start)
        pl.when(j == Z - 1)(n3_start)

        @pl.when(j < Z)
        def _():
            r = at(zz, x)
            t3_wait(r, t3_r)
            process(r)

        @pl.when(j >= 1)
        def _():
            for o in range(1, X):
                r = at(nearest(j - 1), other_x(o))
                pltpu.make_async_copy(cbuf.at[r], cbuf.at[r], c_rs.at[r]).wait()
                t3_wait(r, t3_r)
                process(r)

        return carry

    lax.fori_loop(0, Z + 1, step, 0)

    def gm(o):
        return remote(gmp.at[m], gmp.at[m], gm_s.at[o], gm_r.at[o], me, other_m(o))

    def gr(o):
        return remote(grep.at[me], grep.at[me], gr_s.at[o], gr_r.at[o], other_r(o), m)

    gmp[m] = gloc[...]
    for o in range(1, M):
        gm(o).start()
    for o in range(1, M):
        gm(o).wait_recv()
    total = gmp[0]
    for o in range(1, M):
        total = total + gmp[o]
    grep[me] = total
    for o in range(1, R):
        gr(o).start()
    for o in range(1, R):
        gr(o).wait_recv()
    gram = grep[0]
    for o in range(1, R):
        gram = gram + grep[o]

    sub = lax.broadcasted_iota(jnp.int32, (grows, LANES), 0)
    lane = lax.broadcasted_iota(jnp.int32, (grows, LANES), 1)
    lane1 = lax.broadcasted_iota(jnp.int32, (1, LANES), 1)
    coef = jnp.ones((1, LANES), F32)
    count = R
    while count > 1:
        half = count // 2
        inside = (sub < count) & (lane < count)
        gram = jnp.where(inside, gram, 0.0)
        diagonal = jnp.where(sub == lane, gram, 0.0)
        crossed = jnp.where((sub == lane + half) | (lane == sub + half), gram, 0.0)
        factors = []
        for axis in (0, 1):
            square = jnp.sum(diagonal, axis=axis, keepdims=True)
            cross = jnp.sum(crossed, axis=axis, keepdims=True)
            factors.append(1.0 - cross / (2.0 * square + eps))
        scaled = jnp.where(inside, factors[0] * gram * factors[1], 0.0)
        scaled = scaled + pltpu.roll(scaled, LANES - half, 1)
        gram = scaled + pltpu.roll(scaled, grows - half, 0)
        along = jnp.broadcast_to(jnp.where(lane1 < count, factors[0], 0.0), (8, LANES))
        reach = count
        while reach < R:
            along = along + pltpu.roll(along, reach, 1)
            reach *= 2
        coef = coef * along[:1]
        count = half
    weights = [
        jnp.sum(jnp.where(lane1 == r, coef, 0.0), axis=1, keepdims=True) for r in range(R)
    ]

    own[3].wait()
    tall = 16

    def w_rows(xx):
        return aligned(xx, rows)

    def w_across(b, o):
        piece = wbuf.at[w_rows(x), aligned(b, width)]
        return remote(piece, piece, w_s.at[b, o], w_r.at[b, x], at(z, other_x(o)), m)

    def update(b, carry):
        at_cols = aligned(b, width)

        def row(i, inner):
            at_rows = aligned(i, tall)
            total = weights[0] * grads[0, at_rows, at_cols]
            for r in range(1, R):
                total = total + weights[r] * grads[r, at_rows, at_cols]
            new = wown[at_rows, at_cols].astype(F32) - learning_rate * total
            wbuf[pl.ds(pl.multiple_of(x * rows + i * tall, tall), tall), at_cols] = new.astype(
                BF16
            )
            return inner

        lax.fori_loop(0, rows // tall, row, 0)
        for o in range(1, X):
            w_across(b, o).start()
        return carry

    lax.fori_loop(0, blocks, update, 0)
    w_out = pltpu.make_async_copy(wbuf.at[w_rows(x), :], wo_hbm, local_sem.at[5])
    w_out.start()

    own[2].wait()
    for o in range(1, Z):
        zz = lax.rem(z + o, Z)
        wait_all(nbuf.at[zz, pl.ds(0, (M - 1) * nq), :], n3_r.at[zz])

    def r_send(dest, b):
        to = jnp.where(dest > z, z + 1, z - 1)
        slot = jnp.where((to == dest) & (dest < z), Z, dest)
        at_cols = aligned(b, width)
        return remote(
            rsend.at[dest, :, at_cols],
            rrecv.at[slot, :, at_cols],
            rs_s.at[dest, b],
            rs_r.at[slot, b],
            at(to, x),
            m,
        )

    def r_wait(slot, b):
        piece = rrecv.at[slot, :, aligned(b, width)]
        pltpu.make_async_copy(piece, piece, rs_r.at[slot, b]).wait()

    scale = cols * M

    def product(b, carry):
        at_cols = aligned(b, width)
        for o in range(1, X):
            xx = other_x(o)
            piece = wbuf.at[w_rows(xx), at_cols]
            pltpu.make_async_copy(piece, piece, w_r.at[b, xx]).wait()

        def one(dest, inner):
            part[dest] = jnp.dot(nbuf[dest], wbuf[:, at_cols], preferred_element_type=F32)
            return inner

        lax.fori_loop(0, Z, one, 0)
        for i in range(Z - 1, 0, -1):
            dest = nearest(i)
            before = jnp.where(dest > z, z - 1, z + 1)
            more = (before >= 0) & (before < Z)

            @pl.when(more)
            def _():
                r_wait(dest, b)
                rsend[dest, :, at_cols] = (
                    part[dest] + rrecv[dest, :, at_cols].astype(F32)
                ).astype(BF16)

            @pl.when(jnp.logical_not(more))
            def _():
                rsend[dest, :, at_cols] = part[dest].astype(BF16)

            r_send(dest, b).start()

        @pl.when(z > 0)
        def _():
            r_wait(z, b)
            part[z] = part[z] + rrecv[z, :, at_cols].astype(F32)

        @pl.when(z < Z - 1)
        def _():
            r_wait(Z, b)
            part[z] = part[z] + rrecv[Z, :, at_cols].astype(F32)

        qbuf[:, at_cols] = (part[z] * scale**-0.5).astype(BF16)
        return carry

    lax.fori_loop(0, blocks, product, 0)
    q_out = pltpu.make_async_copy(qbuf, q_hbm, local_sem.at[6])
    q_out.start()

    pl.when(z < Z - 1)(lambda: c_up().wait_send())
    pl.when(z > 0)(lambda: c_down().wait_send())
    for o in range(1, X):
        for j in range(Z):
            c_across(j, o).wait_send()
    for j in range(1, Z):
        ok, copy = c_forward(j)
        pl.when(ok)(lambda copy=copy: copy().wait_send())
    for o in range(1, M):
        t1(o).wait_send()
        gm(o).wait_send()
    for o in range(1, R):
        t2(o).wait_send()
        gr(o).wait_send()
    for r in range(R):
        t3_wait(r, t3_s)
    for o in range(1, Z):
        n2(o).wait_send()
        zz = lax.rem(z + o, Z)
        wait_all(nbuf.at[zz, pl.ds(0, (M - 1) * nq), :], n3_s.at[zz])
    for b in range(blocks):
        for o in range(1, X):
            w_across(b, o).wait_send()
        for i in range(1, Z):
            r_send(nearest(i), b).wait_send()
    w_out.wait()
    q_out.wait()


def local(weight, tokens, cotangent, next_tokens):
    R = lax.axis_size("rep")
    M = lax.axis_size("mp")
    X = x_size(R)
    Z = R // X
    tok, cols = cotangent.shape
    rows = weight.shape[0]
    ntok = next_tokens.shape[0]
    width = min(256, cols)
    blocks = cols // width
    grows = max(8, R)
    dma = pltpu.SemaphoreType.DMA
    anywhere = pl.BlockSpec(memory_space=pl.ANY)
    return pl.pallas_call(
        functools.partial(kernel, (Z, X, M, width)),
        out_shape=(
            jax.ShapeDtypeStruct((rows, cols), BF16),
            jax.ShapeDtypeStruct((ntok, cols), BF16),
        ),
        in_specs=[anywhere] * 4,
        out_specs=(anywhere, anywhere),
        scratch_shapes=[
            pltpu.VMEM((R, tok, cols), BF16),
            pltpu.VMEM((M, tok // M, cols), BF16),
            pltpu.VMEM((R, tok, rows), BF16),
            pltpu.VMEM((rows, tok), BF16),
            pltpu.VMEM((Z, ntok, X * rows), BF16),
            pltpu.VMEM((R, rows, cols), F32),
            pltpu.VMEM((grows, LANES), F32),
            pltpu.VMEM((M, grows, LANES), F32),
            pltpu.VMEM((R, grows, LANES), F32),
            pltpu.VMEM((rows, cols), BF16),
            pltpu.VMEM((X * rows, cols), BF16),
            pltpu.VMEM((Z, ntok, width), F32),
            pltpu.VMEM((Z, ntok, cols), BF16),
            pltpu.VMEM((Z + 1, ntok, cols), BF16),
            pltpu.VMEM((ntok, cols), BF16),
            dma((7,)),
            dma((2,)),
            dma((Z,)),
            dma((Z, X)),
            dma((R,)),
            dma((M,)),
            dma((M,)),
            dma((R,)),
            dma((R,)),
            dma((R,)),
            dma((R,)),
            dma((Z,)),
            dma((Z,)),
            dma((Z,)),
            dma((Z,)),
            dma((M,)),
            dma((M,)),
            dma((R,)),
            dma((R,)),
            dma((blocks, X)),
            dma((blocks, X)),
            dma((Z, blocks)),
            dma((Z + 1, blocks)),
        ],
        compiler_params=pltpu.CompilerParams(
            collective_id=0, has_side_effects=True, vmem_limit_bytes=60 * 1024 * 1024
        ),
    )(weight, tokens, cotangent, next_tokens)


def solution(mesh):
    in_specs = (P("rep", "mp"), P("rep", "mp"), P("rep", "mp"), P("rep", None))
    out_specs = (P("rep", "mp"), P("rep", "mp"))
    return jax.shard_map(local, mesh=mesh, in_specs=in_specs, out_specs=out_specs, check_vma=False)
```

```python
import functools

import jax
import jax.numpy as jnp
from jax import lax
from jax.experimental import pallas as pl
from jax.experimental.pallas import tpu as pltpu
from jax.sharding import PartitionSpec as P

learning_rate = 0.002
eps = 1e-06
F32 = jnp.float32
BF16 = jnp.bfloat16
MESH = pl.DeviceIdType.MESH
LANES = 128


def x_size(replicas):
    x = 1
    while 2 * (2 * x) ** 2 <= replicas and replicas % (2 * x) == 0:
        x *= 2
    return x


def aligned(start, size):
    return pl.ds(pl.multiple_of(start * size, size), size)


def kernel(
    sizes,
    w_hbm,
    t_hbm,
    c_hbm,
    n_hbm,
    wo_hbm,
    q_hbm,
    cbuf,
    t1buf,
    tfull,
    ttr,
    nbuf,
    grads,
    gloc,
    gmp,
    grep,
    wown,
    wbuf,
    part,
    qsum,
    rsend,
    rrecv,
    qbuf,
    local_sem,
    c_own,
    c_fwd,
    c_xs,
    c_rs,
    t1_s,
    t1_r,
    t2_s,
    t2_r,
    t3_s,
    t3_r,
    n2_s,
    n2_r,
    n3_s,
    n3_r,
    gm_s,
    gm_r,
    gr_s,
    gr_r,
    w_s,
    w_r,
    rs_s,
    rs_r,
):
    Z, X, M, width = sizes
    R = Z * X
    _, parts, tok, piece_cols = cbuf.shape
    cols = parts * piece_cols
    rows = tfull.shape[2]
    feats = X * rows
    tq = tok // M
    ntok = nbuf.shape[1]
    nq = ntok // M
    blocks = cols // width
    group = min(8, R)
    grows = gloc.shape[0]

    me = lax.axis_index("rep")
    m = lax.axis_index("mp")
    z = me // X
    x = lax.rem(me, X)

    def nearest(j):
        found = jnp.int32(0)
        for a in range(Z):
            order = sorted(range(Z), key=lambda b: (abs(b - a), b))
            for i in range(Z):
                found = found + jnp.where((z == a) & (j == i), order[i], 0)
        return found

    def remote(src, dst, send, recv, r, mm):
        return pltpu.make_async_remote_copy(
            src_ref=src,
            dst_ref=dst,
            send_sem=send,
            recv_sem=recv,
            device_id=(r, mm),
            device_id_type=MESH,
        )

    def arrived(piece, sem):
        pltpu.make_async_copy(piece, piece, sem).wait()

    def other_x(o):
        return lax.rem(x + o, X)

    def other_m(o):
        return lax.rem(m + o, M)

    def other_r(o):
        return lax.rem(me + o, R)

    def at(zz, xx):
        return zz * X + xx

    def c_mine(h):
        return c_hbm.at[:, aligned(h, piece_cols)]

    def own_copies():
        copies = [
            pltpu.make_async_copy(c_mine(h), cbuf.at[me, h], local_sem.at[5 + h])
            for h in range(parts)
        ]
        own_tokens = t1buf.at[:, aligned(m, cols)]
        return [
            pltpu.make_async_copy(n_hbm.at[:, aligned(z, feats)], nbuf.at[z], local_sem.at[0]),
            pltpu.make_async_copy(w_hbm, wown, local_sem.at[1]),
            pltpu.make_async_copy(t_hbm.at[aligned(m, tq), :], own_tokens, local_sem.at[2]),
        ] + copies

    for copy in own_copies():
        copy.start()

    barrier = pltpu.get_barrier_semaphore()
    for o in range(1, M):
        pl.semaphore_signal(barrier, inc=1, device_id=(me, other_m(o)), device_id_type=MESH)
    for o in range(1, R):
        pl.semaphore_signal(barrier, inc=1, device_id=(other_r(o), m), device_id_type=MESH)
    pl.semaphore_wait(barrier, M + R - 2)

    def t1(o):
        mm = other_m(o)
        return remote(
            t_hbm.at[aligned(mm, tq), :],
            t1buf.at[:, aligned(m, cols)],
            t1_s.at[o],
            t1_r.at[o],
            me,
            mm,
        )

    for o in range(1, M):
        t1(o).start()

    def c_up(h):
        return remote(
            c_mine(h), cbuf.at[me, h], c_own.at[0, h], c_rs.at[me, h], at(z + 1, x), m
        )

    def c_down(h):
        return remote(
            c_mine(h), cbuf.at[me, h], c_own.at[1, h], c_rs.at[me, h], at(z - 1, x), m
        )

    def c_across(j, h, o):
        r = at(nearest(j), x)
        here = cbuf.at[r, h]
        return remote(here, here, c_xs.at[j, h, o], c_rs.at[r, h], at(z, other_x(o)), m)

    def c_forward(j, h):
        zz = nearest(j)
        r = at(zz, x)
        to = jnp.where(zz < z, z + 1, z - 1)
        here = cbuf.at[r, h]
        return (
            (to >= 0) & (to < Z),
            lambda: remote(here, here, c_fwd.at[j, h], c_rs.at[r, h], at(to, x), m),
        )

    own = own_copies()
    for h in range(parts):
        pl.when(z < Z - 1)(lambda h=h: c_up(h).start())
        pl.when(z > 0)(lambda h=h: c_down(h).start())
        own[3 + h].wait()
        for o in range(1, X):
            c_across(0, h, o).start()

    def zero(i, carry):
        for r in range(R):
            grads[r, aligned(i, 8), :] = jnp.zeros((8, cols), F32)
        return carry

    lax.fori_loop(0, rows // 8, zero, 0)
    gloc[...] = jnp.zeros_like(gloc)

    own[2].wait()
    for o in range(1, M):
        t1(o).wait_recv()

    def t2(j, o):
        r = at(nearest(j), other_x(o))
        return remote(
            t1buf.at[:, aligned(r, rows)],
            tfull.at[me, aligned(m, tq), :],
            t2_s.at[j * X + o],
            t2_r.at[me],
            r,
            m,
        )

    mine = tfull.at[me, aligned(m, tq), :]
    pltpu.make_async_copy(t1buf.at[:, aligned(me, rows)], mine, t2_r.at[me]).start()
    for j in range(Z):
        for o in range(1 if j == 0 else 0, X):
            t2(j, o).start()

    def t3(r, o):
        here = tfull.at[r, aligned(m, tq), :]
        return remote(here, here, t3_s.at[r], t3_r.at[r], me, other_m(o))

    def t3_start(j):
        for xo in range(X):
            r = at(nearest(j), other_x(xo))
            arrived(tfull.at[r, aligned(m, tq), :], t2_r.at[r])
            for o in range(1, M):
                t3(r, o).start()

    def t3_wait(r, sem):
        arrived(tfull.at[r, pl.ds(0, (M - 1) * tq), :], sem.at[r])

    def pass_cotangent(j):
        r = at(nearest(j), x)
        for h in range(parts):
            arrived(cbuf.at[r, h], c_rs.at[r, h])
            ok, copy = c_forward(j, h)
            pl.when(ok)(lambda copy=copy: copy().start())
            for o in range(1, X):
                c_across(j, h, o).start()

    lead = min(2, Z)
    for j in range(lead):
        if j > 0:
            pass_cotangent(j)
        t3_start(j)

    def n2(i):
        zz = nearest(i)
        return remote(
            n_hbm.at[aligned(m, nq), aligned(zz, feats)],
            nbuf.at[z, aligned(m, nq), :],
            n2_s.at[i],
            n2_r.at[z],
            at(zz, x),
            m,
        )

    def n3(zz, o):
        here = nbuf.at[zz, aligned(m, nq), :]
        return remote(here, here, n3_s.at[zz], n3_r.at[zz], me, other_m(o))

    def n2_start():
        for i in range(Z - 1, 0, -1):
            n2(i).start()

    def n3_start(i):
        zz = nearest(i)
        here = nbuf.at[zz, aligned(m, nq), :]
        arrived(here, n2_r.at[zz])
        for p in range(1, M):
            n3(zz, p).start()

    def n3_wait(zz, sem):
        arrived(nbuf.at[zz, pl.ds(0, (M - 1) * nq), :], sem.at[zz])

    def turn(r):
        t3_wait(r, t3_r)
        ttr[r] = tfull[r].T

    def process(r, h):
        tile = min(256, piece_cols)

        def grad_tile(i, carry):
            at_cols = pl.ds(pl.multiple_of(h * piece_cols + i * tile, tile), tile)
            grads[r, :, at_cols] = jnp.dot(
                ttr[r], cbuf[r, h, :, aligned(i, tile)], preferred_element_type=F32
            )
            return carry

        lax.fori_loop(0, piece_cols // tile, grad_tile, 0)
        high = min(32, rows)
        sub = lax.broadcasted_iota(jnp.int32, gloc.shape, 0)
        lane = lax.broadcasted_iota(jnp.int32, gloc.shape, 1)

        def dots(g, carry):
            def row(i, sums):
                at_rows = aligned(i, high)
                at_cols = aligned(h, piece_cols)
                new = grads[r, at_rows, at_cols]
                out = []
                for q in range(group):
                    prod = new * grads[g * group + q, at_rows, at_cols]
                    terms = [
                        prod[k * 8 : k * 8 + 8, a * LANES : (a + 1) * LANES]
                        for k in range(high // 8)
                        for a in range(piece_cols // LANES)
                    ]
                    while len(terms) > 1:
                        terms = [
                            sum(terms[k + 1 : k + 2], terms[k]) for k in range(0, len(terms), 2)
                        ]
                    out.append(sums[q] + terms[0])
                return tuple(out)

            sums = lax.fori_loop(
                0, rows // high, row, tuple(jnp.zeros((8, LANES), F32) for _ in range(group))
            )
            gram = gloc[...]
            for q in range(group):
                other = g * group + q
                total = jnp.sum(jnp.sum(sums[q], axis=1, keepdims=True), axis=0, keepdims=True)
                here = ((sub == r) & (lane == other)) | ((sub == other) & (lane == r))
                gram = gram + jnp.where(here, total, 0.0)
            gloc[...] = gram
            return carry

        lax.fori_loop(0, R // group, dots, 0)

    def step(j, carry):
        zz = nearest(j)

        @pl.when((j >= lead - 1) & (j < Z - 1))
        def _():
            pass_cotangent(j + 1)
            t3_start(j + 1)

        pl.when(j == max(Z - 2, 0))(n2_start)
        if Z > 1:
            pl.when(j == Z)(lambda: n3_start(Z - 1))

        @pl.when(j < Z)
        def _():
            r = at(zz, x)
            for o in range(X):
                turn(at(zz, other_x(o)))

            def one(h, inner):
                process(r, h)
                return inner

            lax.fori_loop(0, parts, one, 0)

        @pl.when(j >= 1)
        def _():
            for o in range(1, X):
                r = at(nearest(j - 1), other_x(o))

                def one(h, inner):
                    arrived(cbuf.at[r, h], c_rs.at[r, h])
                    process(r, h)
                    return inner

                lax.fori_loop(0, parts, one, 0)

        return carry

    lax.fori_loop(0, Z + 1, step, 0)

    def gm(o):
        return remote(gmp.at[m], gmp.at[m], gm_s.at[o], gm_r.at[o], me, other_m(o))

    def gr(o):
        return remote(grep.at[me], grep.at[me], gr_s.at[o], gr_r.at[o], other_r(o), m)

    gmp[m] = gloc[...]
    for o in range(1, M):
        gm(o).start()
    for i in range(Z - 2, 0, -1):
        n3_start(i)
    for o in range(1, M):
        gm(o).wait_recv()
    total = gmp[0]
    for o in range(1, M):
        total = total + gmp[o]
    grep[me] = total
    for o in range(1, R):
        gr(o).start()
    for o in range(1, R):
        gr(o).wait_recv()
    gram = grep[0]
    for o in range(1, R):
        gram = gram + grep[o]

    sub = lax.broadcasted_iota(jnp.int32, (grows, LANES), 0)
    lane = lax.broadcasted_iota(jnp.int32, (grows, LANES), 1)
    lane1 = lax.broadcasted_iota(jnp.int32, (1, LANES), 1)
    coef = jnp.ones((1, LANES), F32)
    count = R
    while count > 1:
        half = count // 2
        inside = (sub < count) & (lane < count)
        gram = jnp.where(inside, gram, 0.0)
        diagonal = jnp.where(sub == lane, gram, 0.0)
        crossed = jnp.where((sub == lane + half) | (lane == sub + half), gram, 0.0)
        factors = []
        for axis in (0, 1):
            square = jnp.sum(diagonal, axis=axis, keepdims=True)
            cross = jnp.sum(crossed, axis=axis, keepdims=True)
            factors.append(1.0 - cross / (2.0 * square + eps))
        scaled = jnp.where(inside, factors[0] * gram * factors[1], 0.0)
        scaled = scaled + pltpu.roll(scaled, LANES - half, 1)
        gram = scaled + pltpu.roll(scaled, grows - half, 0)
        along = jnp.broadcast_to(jnp.where(lane1 < count, factors[0], 0.0), (8, LANES))
        reach = count
        while reach < R:
            along = along + pltpu.roll(along, reach, 1)
            reach *= 2
        coef = coef * along[:1]
        count = half
    weights = [
        jnp.sum(jnp.where(lane1 == r, coef, 0.0), axis=1, keepdims=True) for r in range(R)
    ]

    own[1].wait()
    tall = min(64, rows)

    def w_rows(xx):
        return aligned(xx, rows)

    def w_across(b, o):
        piece = wbuf.at[w_rows(x), aligned(b, width)]
        return remote(piece, piece, w_s.at[b, o], w_r.at[b, x], at(z, other_x(o)), m)

    def update(b, carry):
        at_cols = aligned(b, width)

        def row(i, inner):
            at_rows = aligned(i, tall)
            total = weights[0] * grads[0, at_rows, at_cols]
            for r in range(1, R):
                total = total + weights[r] * grads[r, at_rows, at_cols]
            new = wown[at_rows, at_cols].astype(F32) - learning_rate * total
            wbuf[pl.ds(pl.multiple_of(x * rows + i * tall, tall), tall), at_cols] = new.astype(
                BF16
            )
            return inner

        lax.fori_loop(0, rows // tall, row, 0)
        for o in range(1, X):
            w_across(b, o).start()
        return carry

    lax.fori_loop(0, blocks, update, 0)
    w_out = pltpu.make_async_copy(wbuf.at[w_rows(x), :], wo_hbm, local_sem.at[3])
    w_out.start()

    def r_send(dest, b):
        to = jnp.where(dest > z, z + 1, z - 1)
        slot = jnp.where((to == dest) & (dest < z), Z, dest)
        at_cols = aligned(b, width)
        return remote(
            rsend.at[dest, :, at_cols],
            rrecv.at[slot, :, at_cols],
            rs_s.at[dest, b],
            rs_r.at[slot, b],
            at(to, x),
            m,
        )

    def r_wait(slot, b):
        piece = rrecv.at[slot, :, aligned(b, width)]
        arrived(piece, rs_r.at[slot, b])

    scale = cols * M

    def product(dest, b):
        return jnp.dot(nbuf[dest], wbuf[:, aligned(b, width)], preferred_element_type=F32)

    def pass_on(dest, b):
        at_cols = aligned(b, width)
        before = jnp.where(dest > z, z - 1, z + 1)
        more = (before >= 0) & (before < Z)
        part[...] = product(dest, b)

        @pl.when(more)
        def _():
            r_wait(dest, b)
            rsend[dest, :, at_cols] = (part[...] + rrecv[dest, :, at_cols].astype(F32)).astype(
                BF16
            )

        @pl.when(jnp.logical_not(more))
        def _():
            rsend[dest, :, at_cols] = part[...].astype(BF16)

        r_send(dest, b).start()

    def far(b, carry):
        for o in range(1, X):
            xx = other_x(o)
            arrived(wbuf.at[w_rows(xx), aligned(b, width)], w_r.at[b, xx])

        def one(i, inner):
            dest = nearest(Z - 1 - i)
            wanted = jnp.abs(dest - z) >= 2
            pl.when(wanted & (b == 0))(lambda: n3_wait(dest, n3_r))
            pl.when(wanted)(lambda: pass_on(dest, b))
            return inner

        return lax.fori_loop(0, Z - 1, one, carry)

    def near(b, carry):
        def one(i, inner):
            dest = nearest(Z - 1 - i)
            wanted = jnp.abs(dest - z) == 1
            pl.when(wanted & (b == 0))(lambda: n3_wait(dest, n3_r))
            pl.when(wanted)(lambda: pass_on(dest, b))
            return inner

        return lax.fori_loop(0, Z - 1, one, carry)

    def stay(b, carry):
        qsum[:, aligned(b, width)] = product(z, b)
        return carry

    def finish(b, carry):
        at_cols = aligned(b, width)

        @pl.when(z > 0)
        def _():
            r_wait(z, b)
            qsum[:, at_cols] = qsum[:, at_cols] + rrecv[z, :, at_cols].astype(F32)

        @pl.when(z < Z - 1)
        def _():
            r_wait(Z, b)
            qsum[:, at_cols] = qsum[:, at_cols] + rrecv[Z, :, at_cols].astype(F32)

        qbuf[:, at_cols] = (qsum[:, at_cols] * scale**-0.5).astype(BF16)
        return carry

    lax.fori_loop(0, blocks, far, 0)
    lax.fori_loop(0, blocks, near, 0)
    own[0].wait()
    lax.fori_loop(0, blocks, stay, 0)
    lax.fori_loop(0, blocks, finish, 0)
    q_out = pltpu.make_async_copy(qbuf, q_hbm, local_sem.at[4])
    q_out.start()

    for h in range(parts):
        pl.when(z < Z - 1)(lambda h=h: c_up(h).wait_send())
        pl.when(z > 0)(lambda h=h: c_down(h).wait_send())
        for j in range(Z):
            for o in range(1, X):
                c_across(j, h, o).wait_send()
        for j in range(1, Z):
            ok, copy = c_forward(j, h)
            pl.when(ok)(lambda copy=copy: copy().wait_send())
    for j in range(Z):
        for o in range(1 if j == 0 else 0, X):
            t2(j, o).wait_send()
    for o in range(1, M):
        gm(o).wait_send()
    for o in range(1, R):
        gr(o).wait_send()
    for o in range(1, M):
        t1(o).wait_send()
    for r in range(R):
        t3_wait(r, t3_s)
    for i in range(1, Z):
        n2(i).wait_send()
        n3_wait(nearest(i), n3_s)
    for b in range(blocks):
        for o in range(1, X):
            w_across(b, o).wait_send()
        for i in range(1, Z):
            r_send(nearest(i), b).wait_send()
    w_out.wait()
    q_out.wait()


def local(weight, tokens, cotangent, next_tokens):
    R = lax.axis_size("rep")
    M = lax.axis_size("mp")
    X = x_size(R)
    Z = R // X
    tok, cols = cotangent.shape
    rows = weight.shape[0]
    ntok = next_tokens.shape[0]
    width = min(256, cols)
    parts = 2 if cols % (2 * LANES) == 0 else 1
    blocks = cols // width
    grows = max(8, R)
    dma = pltpu.SemaphoreType.DMA
    anywhere = pl.BlockSpec(memory_space=pl.ANY)
    return pl.pallas_call(
        functools.partial(kernel, (Z, X, M, width)),
        out_shape=(
            jax.ShapeDtypeStruct((rows, cols), BF16),
            jax.ShapeDtypeStruct((ntok, cols), BF16),
        ),
        in_specs=[anywhere] * 4,
        out_specs=(anywhere, anywhere),
        scratch_shapes=[
            pltpu.VMEM((R, parts, tok, cols // parts), BF16),
            pltpu.VMEM((tok // M, M * cols), BF16),
            pltpu.VMEM((R, tok, rows), BF16),
            pltpu.VMEM((R, rows, tok), BF16),
            pltpu.VMEM((Z, ntok, X * rows), BF16),
            pltpu.VMEM((R, rows, cols), F32),
            pltpu.VMEM((grows, LANES), F32),
            pltpu.VMEM((M, grows, LANES), F32),
            pltpu.VMEM((R, grows, LANES), F32),
            pltpu.VMEM((rows, cols), BF16),
            pltpu.VMEM((X * rows, cols), BF16),
            pltpu.VMEM((ntok, width), F32),
            pltpu.VMEM((ntok, cols), F32),
            pltpu.VMEM((Z, ntok, cols), BF16),
            pltpu.VMEM((Z + 1, ntok, cols), BF16),
            pltpu.VMEM((ntok, cols), BF16),
            dma((5 + parts,)),
            dma((2, parts)),
            dma((Z, parts)),
            dma((Z, parts, X)),
            dma((R, parts)),
            dma((M,)),
            dma((M,)),
            dma((R,)),
            dma((R,)),
            dma((R,)),
            dma((R,)),
            dma((Z,)),
            dma((Z,)),
            dma((Z,)),
            dma((Z,)),
            dma((M,)),
            dma((M,)),
            dma((R,)),
            dma((R,)),
            dma((blocks, X)),
            dma((blocks, X)),
            dma((Z, blocks)),
            dma((Z + 1, blocks)),
        ],
        compiler_params=pltpu.CompilerParams(
            collective_id=0, has_side_effects=True, vmem_limit_bytes=60 * 1024 * 1024
        ),
    )(weight, tokens, cotangent, next_tokens)


def solution(mesh):
    in_specs = (P("rep", "mp"), P("rep", "mp"), P("rep", "mp"), P("rep", None))
    out_specs = (P("rep", "mp"), P("rep", "mp"))
    return jax.shard_map(local, mesh=mesh, in_specs=in_specs, out_specs=out_specs, check_vma=False)
```

```python
import functools

import jax
import jax.numpy as jnp
from jax import lax
from jax.experimental import pallas as pl
from jax.experimental.pallas import tpu as pltpu
from jax.sharding import PartitionSpec as P

learning_rate = 0.002
eps = 1e-06
F32 = jnp.float32
BF16 = jnp.bfloat16
MESH = pl.DeviceIdType.MESH
LANES = 128


def x_size(replicas):
    x = 1
    while 2 * (2 * x) ** 2 <= replicas and replicas % (2 * x) == 0:
        x *= 2
    return x


def aligned(start, size):
    return pl.ds(pl.multiple_of(start * size, size), size)


def kernel(
    sizes,
    w_hbm,
    t_hbm,
    c_hbm,
    n_hbm,
    wo_hbm,
    q_hbm,
    cbuf,
    t1buf,
    tfull,
    ttr,
    nbuf,
    grads,
    gloc,
    gmp,
    grep,
    wown,
    wbuf,
    part,
    qsum,
    rsend,
    rrecv,
    qbuf,
    local_sem,
    c_own,
    c_fwd,
    c_xs,
    c_rs,
    t1_s,
    t1_r,
    t2_s,
    t2_r,
    t3_s,
    t3_r,
    n2_s,
    n2_r,
    n3_s,
    n3_r,
    n4_s,
    n4_r,
    gm_s,
    gm_r,
    gr_s,
    gr_r,
    w_s,
    w_r,
    rs_s,
    rs_r,
):
    Z, X, M, width = sizes
    R = Z * X
    _, parts, tok, piece_cols = cbuf.shape
    cols = parts * piece_cols
    rows = tfull.shape[2]
    feats = X * rows
    tq = tok // M
    ntok = nbuf.shape[1]
    nq = ntok // M
    blocks = cols // width
    group = min(8, R)
    grows = gloc.shape[0]

    me = lax.axis_index("rep")
    m = lax.axis_index("mp")
    z = me // X
    x = lax.rem(me, X)

    def nearest(j):
        found = jnp.int32(0)
        for a in range(Z):
            order = sorted(range(Z), key=lambda b: (abs(b - a), b))
            for i in range(Z):
                found = found + jnp.where((z == a) & (j == i), order[i], 0)
        return found

    def remote(src, dst, send, recv, r, mm):
        return pltpu.make_async_remote_copy(
            src_ref=src,
            dst_ref=dst,
            send_sem=send,
            recv_sem=recv,
            device_id=(r, mm),
            device_id_type=MESH,
        )

    def arrived(piece, sem):
        pltpu.make_async_copy(piece, piece, sem).wait()

    def other_x(o):
        return lax.rem(x + o, X)

    def other_m(o):
        return lax.rem(m + o, M)

    ys = M // 2
    y = m // 2
    core = lax.rem(m, 2)
    partner = y * 2 + 1 - core

    def other_y(i):
        return lax.rem(y + i, ys) * 2 + core

    def from_y(i):
        return lax.rem(y + ys - i, ys) * 2 + core

    def other_r(o):
        return lax.rem(me + o, R)

    def at(zz, xx):
        return zz * X + xx

    def c_mine(h):
        return c_hbm.at[:, aligned(h, piece_cols)]

    def own_copies():
        copies = [
            pltpu.make_async_copy(c_mine(h), cbuf.at[me, h], local_sem.at[5 + h])
            for h in range(parts)
        ]
        own_tokens = t1buf.at[:, aligned(m, cols)]
        return [
            pltpu.make_async_copy(n_hbm.at[:, aligned(z, feats)], nbuf.at[z], local_sem.at[0]),
            pltpu.make_async_copy(w_hbm, wown, local_sem.at[1]),
            pltpu.make_async_copy(t_hbm.at[aligned(m, tq), :], own_tokens, local_sem.at[2]),
        ] + copies

    for copy in own_copies():
        copy.start()

    barrier = pltpu.get_barrier_semaphore()
    for o in range(1, M):
        pl.semaphore_signal(barrier, inc=1, device_id=(me, other_m(o)), device_id_type=MESH)
    for o in range(1, R):
        pl.semaphore_signal(barrier, inc=1, device_id=(other_r(o), m), device_id_type=MESH)
    pl.semaphore_wait(barrier, M + R - 2)

    def t1(o):
        mm = other_m(o)
        return remote(
            t_hbm.at[aligned(mm, tq), :],
            t1buf.at[:, aligned(m, cols)],
            t1_s.at[o],
            t1_r.at[o],
            me,
            mm,
        )

    for o in range(1, M):
        t1(o).start()

    def c_up(h):
        return remote(
            c_mine(h), cbuf.at[me, h], c_own.at[0, h], c_rs.at[me, h], at(z + 1, x), m
        )

    def c_down(h):
        return remote(
            c_mine(h), cbuf.at[me, h], c_own.at[1, h], c_rs.at[me, h], at(z - 1, x), m
        )

    def c_across(j, h, o):
        r = at(nearest(j), x)
        here = cbuf.at[r, h]
        return remote(here, here, c_xs.at[j, h, o], c_rs.at[r, h], at(z, other_x(o)), m)

    def c_forward(j, h):
        zz = nearest(j)
        r = at(zz, x)
        to = jnp.where(zz < z, z + 1, z - 1)
        here = cbuf.at[r, h]
        return (
            (to >= 0) & (to < Z),
            lambda: remote(here, here, c_fwd.at[j, h], c_rs.at[r, h], at(to, x), m),
        )

    own = own_copies()
    for h in range(parts):
        pl.when(z < Z - 1)(lambda h=h: c_up(h).start())
        pl.when(z > 0)(lambda h=h: c_down(h).start())
        own[3 + h].wait()
        for o in range(1, X):
            c_across(0, h, o).start()

    def zero(i, carry):
        for r in range(R):
            grads[r, aligned(i, 8), :] = jnp.zeros((8, cols), F32)
        return carry

    lax.fori_loop(0, rows // 8, zero, 0)
    gloc[...] = jnp.zeros_like(gloc)

    own[2].wait()
    for o in range(1, M):
        t1(o).wait_recv()

    def t2(j, o):
        r = at(nearest(j), other_x(o))
        return remote(
            t1buf.at[:, aligned(r, rows)],
            tfull.at[me, aligned(m, tq), :],
            t2_s.at[j * X + o],
            t2_r.at[me],
            r,
            m,
        )

    mine = tfull.at[me, aligned(m, tq), :]
    pltpu.make_async_copy(t1buf.at[:, aligned(me, rows)], mine, t2_r.at[me]).start()
    for j in range(Z):
        for o in range(1 if j == 0 else 0, X):
            t2(j, o).start()

    def t3(r, o):
        here = tfull.at[r, aligned(m, tq), :]
        return remote(here, here, t3_s.at[r], t3_r.at[r], me, other_m(o))

    def t3_start(j):
        for xo in range(X):
            r = at(nearest(j), other_x(xo))
            arrived(tfull.at[r, aligned(m, tq), :], t2_r.at[r])
            for o in range(1, M):
                t3(r, o).start()

    def t3_wait(r, sem):
        arrived(tfull.at[r, pl.ds(0, (M - 1) * tq), :], sem.at[r])

    def pass_cotangent(j):
        r = at(nearest(j), x)
        for h in range(parts):
            arrived(cbuf.at[r, h], c_rs.at[r, h])
            ok, copy = c_forward(j, h)
            pl.when(ok)(lambda copy=copy: copy().start())
            for o in range(1, X):
                c_across(j, h, o).start()

    def pass_from(distance):
        def one(j, carry):
            pl.when(jnp.abs(nearest(j) - z) == distance)(lambda: pass_cotangent(j))
            return carry

        lax.fori_loop(1, Z, one, 0)

    pass_from(1)
    for j in range(min(2, Z)):
        t3_start(j)

    def n2(i):
        zz = nearest(i)
        return remote(
            n_hbm.at[aligned(m, nq), aligned(zz, feats)],
            nbuf.at[z, aligned(m, nq), :],
            n2_s.at[i],
            n2_r.at[z],
            at(zz, x),
            m,
        )

    def quarter(zz, q):
        return nbuf.at[zz, aligned(q, nq), :]

    def n3_y(zz, i):
        here = quarter(zz, m)
        return remote(here, here, n3_s.at[zz, i], n3_r.at[zz, i], me, other_y(i))

    def n3_core(zz, i):
        here = quarter(zz, m if i == 0 else from_y(i))
        return remote(here, here, n4_s.at[zz, i], n4_r.at[zz, i], me, partner)

    def n2_start():
        for i in range(Z - 1, 0, -1):
            n2(i).start()

    def n3_start(i):
        zz = nearest(i)
        here = nbuf.at[zz, aligned(m, nq), :]
        arrived(here, n2_r.at[zz])
        for i in range(1, ys):
            n3_y(zz, i).start()
        n3_core(zz, 0).start()

    def n3_relay(zz):
        for i in range(1, ys):
            arrived(quarter(zz, m), n3_r.at[zz, i])
            n3_core(zz, i).start()

    def n3_wait(zz):
        for i in range(ys):
            arrived(quarter(zz, m), n4_r.at[zz, i])

    def turn(r):
        t3_wait(r, t3_r)
        ttr[r] = tfull[r].T

    def process(r, h):
        tile = min(256, piece_cols)

        def grad_tile(i, carry):
            at_cols = pl.ds(pl.multiple_of(h * piece_cols + i * tile, tile), tile)
            grads[r, :, at_cols] = jnp.dot(
                ttr[r], cbuf[r, h, :, aligned(i, tile)], preferred_element_type=F32
            )
            return carry

        lax.fori_loop(0, piece_cols // tile, grad_tile, 0)
        high = min(32, rows)
        sub = lax.broadcasted_iota(jnp.int32, gloc.shape, 0)
        lane = lax.broadcasted_iota(jnp.int32, gloc.shape, 1)

        def dots(g, carry):
            def row(i, sums):
                at_rows = aligned(i, high)
                at_cols = aligned(h, piece_cols)
                new = grads[r, at_rows, at_cols]
                out = []
                for q in range(group):
                    prod = new * grads[g * group + q, at_rows, at_cols]
                    terms = [
                        prod[k * 8 : k * 8 + 8, a * LANES : (a + 1) * LANES]
                        for k in range(high // 8)
                        for a in range(piece_cols // LANES)
                    ]
                    while len(terms) > 1:
                        terms = [
                            sum(terms[k + 1 : k + 2], terms[k]) for k in range(0, len(terms), 2)
                        ]
                    out.append(sums[q] + terms[0])
                return tuple(out)

            sums = lax.fori_loop(
                0, rows // high, row, tuple(jnp.zeros((8, LANES), F32) for _ in range(group))
            )
            gram = gloc[...]
            for q in range(group):
                other = g * group + q
                total = jnp.sum(jnp.sum(sums[q], axis=1, keepdims=True), axis=0, keepdims=True)
                here = ((sub == r) & (lane == other)) | ((sub == other) & (lane == r))
                gram = gram + jnp.where(here, total, 0.0)
            gloc[...] = gram
            return carry

        lax.fori_loop(0, R // group, dots, 0)

    def step(j, carry):
        zz = nearest(j)

        @pl.when((j >= 1) & (j < Z - 1))
        def _():
            pass_from(j + 1)

        pl.when((j == 1) & (Z > 2))(lambda: t3_start(2))
        pl.when((j >= 1) & (j < Z - 2))(lambda: t3_start(j + 2))
        pl.when(j == max(Z - 1, 0))(n2_start)

        @pl.when(j < Z)
        def _():
            r = at(zz, x)
            for o in range(X):
                turn(at(zz, other_x(o)))

            def one(h, inner):
                process(r, h)
                return inner

            lax.fori_loop(0, parts, one, 0)

        @pl.when(j >= 1)
        def _():
            for o in range(1, X):
                r = at(nearest(j - 1), other_x(o))

                def one(h, inner):
                    arrived(cbuf.at[r, h], c_rs.at[r, h])
                    process(r, h)
                    return inner

                lax.fori_loop(0, parts, one, 0)

        return carry

    lax.fori_loop(0, Z + 1, step, 0)

    def gm(o):
        return remote(gmp.at[m], gmp.at[m], gm_s.at[o], gm_r.at[o], me, other_m(o))

    def gr(o):
        return remote(grep.at[me], grep.at[me], gr_s.at[o], gr_r.at[o], other_r(o), m)

    gmp[m] = gloc[...]
    for o in range(1, M):
        gm(o).start()
    for i in range(Z - 1, 0, -1):
        n3_start(i)
    for o in range(1, M):
        gm(o).wait_recv()
    total = gmp[0]
    for o in range(1, M):
        total = total + gmp[o]
    grep[me] = total
    for o in range(1, R):
        gr(o).start()
    for o in range(1, R):
        gr(o).wait_recv()
    gram = grep[0]
    for o in range(1, R):
        gram = gram + grep[o]

    sub = lax.broadcasted_iota(jnp.int32, (grows, LANES), 0)
    lane = lax.broadcasted_iota(jnp.int32, (grows, LANES), 1)
    lane1 = lax.broadcasted_iota(jnp.int32, (1, LANES), 1)
    coef = jnp.ones((1, LANES), F32)
    count = R
    while count > 1:
        half = count // 2
        inside = (sub < count) & (lane < count)
        gram = jnp.where(inside, gram, 0.0)
        diagonal = jnp.where(sub == lane, gram, 0.0)
        crossed = jnp.where((sub == lane + half) | (lane == sub + half), gram, 0.0)
        factors = []
        for axis in (0, 1):
            square = jnp.sum(diagonal, axis=axis, keepdims=True)
            cross = jnp.sum(crossed, axis=axis, keepdims=True)
            factors.append(1.0 - cross / (2.0 * square + eps))
        scaled = jnp.where(inside, factors[0] * gram * factors[1], 0.0)
        scaled = scaled + pltpu.roll(scaled, LANES - half, 1)
        gram = scaled + pltpu.roll(scaled, grows - half, 0)
        along = jnp.broadcast_to(jnp.where(lane1 < count, factors[0], 0.0), (8, LANES))
        reach = count
        while reach < R:
            along = along + pltpu.roll(along, reach, 1)
            reach *= 2
        coef = coef * along[:1]
        count = half
    weights = [
        jnp.sum(jnp.where(lane1 == r, coef, 0.0), axis=1, keepdims=True) for r in range(R)
    ]

    own[1].wait()
    tall = min(64, rows)

    def w_rows(xx):
        return aligned(xx, rows)

    def w_across(b, o):
        piece = wbuf.at[w_rows(x), aligned(b, width)]
        return remote(piece, piece, w_s.at[b, o], w_r.at[b, x], at(z, other_x(o)), m)

    def update(b, carry):
        at_cols = aligned(b, width)

        def row(i, inner):
            at_rows = aligned(i, tall)
            total = weights[0] * grads[0, at_rows, at_cols]
            for r in range(1, R):
                total = total + weights[r] * grads[r, at_rows, at_cols]
            new = wown[at_rows, at_cols].astype(F32) - learning_rate * total
            wbuf[pl.ds(pl.multiple_of(x * rows + i * tall, tall), tall), at_cols] = new.astype(
                BF16
            )
            return inner

        lax.fori_loop(0, rows // tall, row, 0)
        for o in range(1, X):
            w_across(b, o).start()
        return carry

    lax.fori_loop(0, blocks, update, 0)
    w_out = pltpu.make_async_copy(wbuf.at[w_rows(x), :], wo_hbm, local_sem.at[3])
    w_out.start()

    def r_send(dest, b):
        to = jnp.where(dest > z, z + 1, z - 1)
        slot = jnp.where((to == dest) & (dest < z), Z, dest)
        at_cols = aligned(b, width)
        return remote(
            rsend.at[dest, :, at_cols],
            rrecv.at[slot, :, at_cols],
            rs_s.at[dest, b],
            rs_r.at[slot, b],
            at(to, x),
            m,
        )

    def r_wait(slot, b):
        piece = rrecv.at[slot, :, aligned(b, width)]
        arrived(piece, rs_r.at[slot, b])

    scale = cols * M

    def product(dest, b):
        return jnp.dot(nbuf[dest], wbuf[:, aligned(b, width)], preferred_element_type=F32)

    def pass_on(dest, b):
        at_cols = aligned(b, width)
        before = jnp.where(dest > z, z - 1, z + 1)
        more = (before >= 0) & (before < Z)
        part[...] = product(dest, b)

        @pl.when(more)
        def _():
            r_wait(dest, b)
            rsend[dest, :, at_cols] = (part[...] + rrecv[dest, :, at_cols].astype(F32)).astype(
                BF16
            )

        @pl.when(jnp.logical_not(more))
        def _():
            rsend[dest, :, at_cols] = part[...].astype(BF16)

        r_send(dest, b).start()

    def far(b, carry):
        for o in range(1, X):
            xx = other_x(o)
            arrived(wbuf.at[w_rows(xx), aligned(b, width)], w_r.at[b, xx])

        def one(i, inner):
            dest = nearest(Z - 1 - i)
            wanted = jnp.abs(dest - z) >= 2
            pl.when(wanted & (b == 0))(lambda: n3_wait(dest))
            pl.when(wanted)(lambda: pass_on(dest, b))
            return inner

        return lax.fori_loop(0, Z - 1, one, carry)

    def near(b, carry):
        def one(i, inner):
            dest = nearest(Z - 1 - i)
            wanted = jnp.abs(dest - z) == 1
            pl.when(wanted & (b == 0))(lambda: n3_wait(dest))
            pl.when(wanted)(lambda: pass_on(dest, b))
            return inner

        return lax.fori_loop(0, Z - 1, one, carry)

    def stay(b, carry):
        qsum[:, aligned(b, width)] = product(z, b)
        return carry

    def finish(b, carry):
        at_cols = aligned(b, width)

        @pl.when(z > 0)
        def _():
            r_wait(z, b)
            qsum[:, at_cols] = qsum[:, at_cols] + rrecv[z, :, at_cols].astype(F32)

        @pl.when(z < Z - 1)
        def _():
            r_wait(Z, b)
            qsum[:, at_cols] = qsum[:, at_cols] + rrecv[Z, :, at_cols].astype(F32)

        qbuf[:, at_cols] = (qsum[:, at_cols] * scale**-0.5).astype(BF16)
        return carry

    for i in range(Z - 1, 0, -1):
        n3_relay(nearest(i))
    lax.fori_loop(0, blocks, far, 0)
    lax.fori_loop(0, blocks, near, 0)
    own[0].wait()
    lax.fori_loop(0, blocks, stay, 0)
    lax.fori_loop(0, blocks, finish, 0)
    q_out = pltpu.make_async_copy(qbuf, q_hbm, local_sem.at[4])
    q_out.start()

    for h in range(parts):
        pl.when(z < Z - 1)(lambda h=h: c_up(h).wait_send())
        pl.when(z > 0)(lambda h=h: c_down(h).wait_send())
        for j in range(Z):
            for o in range(1, X):
                c_across(j, h, o).wait_send()
        for j in range(1, Z):
            ok, copy = c_forward(j, h)
            pl.when(ok)(lambda copy=copy: copy().wait_send())
    for j in range(Z):
        for o in range(1 if j == 0 else 0, X):
            t2(j, o).wait_send()
    for o in range(1, M):
        gm(o).wait_send()
    for o in range(1, R):
        gr(o).wait_send()
    for o in range(1, M):
        t1(o).wait_send()
    for r in range(R):
        t3_wait(r, t3_s)
    for i in range(1, Z):
        n2(i).wait_send()
        zz = nearest(i)
        for k in range(ys):
            if k > 0:
                n3_y(zz, k).wait_send()
            n3_core(zz, k).wait_send()
    for b in range(blocks):
        for o in range(1, X):
            w_across(b, o).wait_send()
        for i in range(1, Z):
            r_send(nearest(i), b).wait_send()
    w_out.wait()
    q_out.wait()


def local(weight, tokens, cotangent, next_tokens):
    R = lax.axis_size("rep")
    M = lax.axis_size("mp")
    X = x_size(R)
    Z = R // X
    tok, cols = cotangent.shape
    rows = weight.shape[0]
    ntok = next_tokens.shape[0]
    width = min(128, cols)
    parts = 2 if cols % (2 * LANES) == 0 else 1
    blocks = cols // width
    grows = max(8, R)
    dma = pltpu.SemaphoreType.DMA
    anywhere = pl.BlockSpec(memory_space=pl.ANY)
    return pl.pallas_call(
        functools.partial(kernel, (Z, X, M, width)),
        out_shape=(
            jax.ShapeDtypeStruct((rows, cols), BF16),
            jax.ShapeDtypeStruct((ntok, cols), BF16),
        ),
        in_specs=[anywhere] * 4,
        out_specs=(anywhere, anywhere),
        scratch_shapes=[
            pltpu.VMEM((R, parts, tok, cols // parts), BF16),
            pltpu.VMEM((tok // M, M * cols), BF16),
            pltpu.VMEM((R, tok, rows), BF16),
            pltpu.VMEM((R, rows, tok), BF16),
            pltpu.VMEM((Z, ntok, X * rows), BF16),
            pltpu.VMEM((R, rows, cols), F32),
            pltpu.VMEM((grows, LANES), F32),
            pltpu.VMEM((M, grows, LANES), F32),
            pltpu.VMEM((R, grows, LANES), F32),
            pltpu.VMEM((rows, cols), BF16),
            pltpu.VMEM((X * rows, cols), BF16),
            pltpu.VMEM((ntok, width), F32),
            pltpu.VMEM((ntok, cols), F32),
            pltpu.VMEM((Z, ntok, cols), BF16),
            pltpu.VMEM((Z + 1, ntok, cols), BF16),
            pltpu.VMEM((ntok, cols), BF16),
            dma((5 + parts,)),
            dma((2, parts)),
            dma((Z, parts)),
            dma((Z, parts, X)),
            dma((R, parts)),
            dma((M,)),
            dma((M,)),
            dma((R,)),
            dma((R,)),
            dma((R,)),
            dma((R,)),
            dma((Z,)),
            dma((Z,)),
            dma((Z, M // 2)),
            dma((Z, M // 2)),
            dma((Z, M // 2)),
            dma((Z, M // 2)),
            dma((M,)),
            dma((M,)),
            dma((R,)),
            dma((R,)),
            dma((blocks, X)),
            dma((blocks, X)),
            dma((Z, blocks)),
            dma((Z + 1, blocks)),
        ],
        compiler_params=pltpu.CompilerParams(
            collective_id=0, has_side_effects=True, vmem_limit_bytes=60 * 1024 * 1024
        ),
    )(weight, tokens, cotangent, next_tokens)


def solution(mesh):
    in_specs = (P("rep", "mp"), P("rep", "mp"), P("rep", "mp"), P("rep", None))
    out_specs = (P("rep", "mp"), P("rep", "mp"))
    return jax.shard_map(local, mesh=mesh, in_specs=in_specs, out_specs=out_specs, check_vma=False)
```

```python
import functools

import jax
import jax.numpy as jnp
from jax import lax
from jax.experimental import pallas as pl
from jax.experimental.pallas import tpu as pltpu
from jax.sharding import PartitionSpec as P

learning_rate = 0.002
eps = 1e-06
F32 = jnp.float32
BF16 = jnp.bfloat16
MESH = pl.DeviceIdType.MESH
LANES = 128


def x_size(replicas):
    x = 1
    while 2 * (2 * x) ** 2 <= replicas and replicas % (2 * x) == 0:
        x *= 2
    return x


def aligned(start, size):
    return pl.ds(pl.multiple_of(start * size, size), size)


def kernel(
    sizes,
    w_hbm,
    t_hbm,
    c_hbm,
    n_hbm,
    wo_hbm,
    q_hbm,
    cbuf,
    t1buf,
    tfull,
    ttr,
    nbuf,
    grads,
    gloc,
    gmp,
    grep,
    wown,
    wbuf,
    part,
    qsum,
    rsend,
    rrecv,
    qbuf,
    local_sem,
    c_own,
    c_fwd,
    c_xs,
    c_rs,
    t1_s,
    t1_r,
    t2_s,
    t2_r,
    t3_s,
    t3_r,
    n2_s,
    n2_r,
    n3_s,
    n3_r,
    n4_s,
    n4_r,
    gm_s,
    gm_r,
    gr_s,
    gr_r,
    w_s,
    w_r,
    rs_s,
    rs_r,
):
    Z, X, M, width = sizes
    R = Z * X
    _, parts, tok, piece_cols = cbuf.shape
    cols = parts * piece_cols
    rows = tfull.shape[2]
    feats = X * rows
    tq = tok // M
    ntok = nbuf.shape[1]
    nq = ntok // M
    blocks = cols // width
    group = min(8, R)
    grows = gloc.shape[0]

    me = lax.axis_index("rep")
    m = lax.axis_index("mp")
    z = me // X
    x = lax.rem(me, X)

    def nearest(j):
        found = jnp.int32(0)
        for a in range(Z):
            order = sorted(range(Z), key=lambda b: (abs(b - a), b))
            for i in range(Z):
                found = found + jnp.where((z == a) & (j == i), order[i], 0)
        return found

    def remote(src, dst, send, recv, r, mm):
        return pltpu.make_async_remote_copy(
            src_ref=src,
            dst_ref=dst,
            send_sem=send,
            recv_sem=recv,
            device_id=(r, mm),
            device_id_type=MESH,
        )

    def arrived(piece, sem):
        pltpu.make_async_copy(piece, piece, sem).wait()

    def other_x(o):
        return lax.rem(x + o, X)

    def other_m(o):
        return lax.rem(m + o, M)

    ys = M // 2
    y = m // 2
    core = lax.rem(m, 2)
    partner = y * 2 + 1 - core

    def other_y(i):
        return lax.rem(y + i, ys) * 2 + core

    def from_y(i):
        return lax.rem(y + ys - i, ys) * 2 + core

    def other_r(o):
        return lax.rem(me + o, R)

    def at(zz, xx):
        return zz * X + xx

    def c_mine(h):
        return c_hbm.at[:, aligned(h, piece_cols)]

    def own_copies():
        copies = [
            pltpu.make_async_copy(c_mine(h), cbuf.at[me, h], local_sem.at[5 + h])
            for h in range(parts)
        ]
        own_tokens = t1buf.at[:, aligned(m, cols)]
        return [
            pltpu.make_async_copy(n_hbm.at[:, aligned(z, feats)], nbuf.at[z], local_sem.at[0]),
            pltpu.make_async_copy(w_hbm, wown, local_sem.at[1]),
            pltpu.make_async_copy(t_hbm.at[aligned(m, tq), :], own_tokens, local_sem.at[2]),
        ] + copies

    for copy in own_copies():
        copy.start()

    barrier = pltpu.get_barrier_semaphore()
    for o in range(1, M):
        pl.semaphore_signal(barrier, inc=1, device_id=(me, other_m(o)), device_id_type=MESH)
    for o in range(1, R):
        pl.semaphore_signal(barrier, inc=1, device_id=(other_r(o), m), device_id_type=MESH)
    pl.semaphore_wait(barrier, M + R - 2)

    def t1(o):
        mm = other_m(o)
        return remote(
            t_hbm.at[aligned(mm, tq), :],
            t1buf.at[:, aligned(m, cols)],
            t1_s.at[o],
            t1_r.at[o],
            me,
            mm,
        )

    for o in range(1, M):
        t1(o).start()

    def c_up(h):
        return remote(
            c_mine(h), cbuf.at[me, h], c_own.at[0, h], c_rs.at[me, h], at(z + 1, x), m
        )

    def c_down(h):
        return remote(
            c_mine(h), cbuf.at[me, h], c_own.at[1, h], c_rs.at[me, h], at(z - 1, x), m
        )

    def c_across(j, h, o):
        r = at(nearest(j), x)
        here = cbuf.at[r, h]
        return remote(here, here, c_xs.at[j, h, o], c_rs.at[r, h], at(z, other_x(o)), m)

    def c_forward(j, h):
        zz = nearest(j)
        r = at(zz, x)
        to = jnp.where(zz < z, z + 1, z - 1)
        here = cbuf.at[r, h]
        return (
            (to >= 0) & (to < Z),
            lambda: remote(here, here, c_fwd.at[j, h], c_rs.at[r, h], at(to, x), m),
        )

    own = own_copies()
    for h in range(parts):
        pl.when(z < Z - 1)(lambda h=h: c_up(h).start())
        pl.when(z > 0)(lambda h=h: c_down(h).start())
        own[3 + h].wait()
        for o in range(1, X):
            c_across(0, h, o).start()

    def zero(i, carry):
        for r in range(R):
            grads[r, aligned(i, 8), :] = jnp.zeros((8, cols), F32)
        return carry

    lax.fori_loop(0, rows // 8, zero, 0)
    gloc[...] = jnp.zeros_like(gloc)

    own[2].wait()
    for o in range(1, M):
        t1(o).wait_recv()

    def t2(j, o):
        r = at(nearest(j), other_x(o))
        return remote(
            t1buf.at[:, aligned(r, rows)],
            tfull.at[me, aligned(m, tq), :],
            t2_s.at[j * X + o],
            t2_r.at[me],
            r,
            m,
        )

    mine = tfull.at[me, aligned(m, tq), :]
    pltpu.make_async_copy(t1buf.at[:, aligned(me, rows)], mine, t2_r.at[me]).start()
    for j in range(Z):
        for o in range(1 if j == 0 else 0, X):
            t2(j, o).start()

    def t3(r, o):
        here = tfull.at[r, aligned(m, tq), :]
        return remote(here, here, t3_s.at[r], t3_r.at[r], me, other_m(o))

    def t3_start(j):
        for xo in range(X):
            r = at(nearest(j), other_x(xo))
            arrived(tfull.at[r, aligned(m, tq), :], t2_r.at[r])
            for o in range(1, M):
                t3(r, o).start()

    def t3_wait(r, sem):
        arrived(tfull.at[r, pl.ds(0, (M - 1) * tq), :], sem.at[r])

    def pass_cotangent(j):
        r = at(nearest(j), x)
        for h in range(parts):
            arrived(cbuf.at[r, h], c_rs.at[r, h])
            ok, copy = c_forward(j, h)
            pl.when(ok)(lambda copy=copy: copy().start())
            for o in range(1, X):
                c_across(j, h, o).start()

    def pass_from(distance):
        def one(j, carry):
            pl.when(jnp.abs(nearest(j) - z) == distance)(lambda: pass_cotangent(j))
            return carry

        lax.fori_loop(1, Z, one, 0)

    pass_from(1)
    for j in range(min(2, Z)):
        t3_start(j)

    def n2(i):
        zz = nearest(i)
        return remote(
            n_hbm.at[aligned(m, nq), aligned(zz, feats)],
            nbuf.at[z, aligned(m, nq), :],
            n2_s.at[i],
            n2_r.at[z],
            at(zz, x),
            m,
        )

    def quarter(zz, q):
        return nbuf.at[zz, aligned(q, nq), :]

    def n3_y(zz, i):
        here = quarter(zz, m)
        return remote(here, here, n3_s.at[zz, i], n3_r.at[zz, i], me, other_y(i))

    def n3_core(zz, i):
        here = quarter(zz, m if i == 0 else from_y(i))
        return remote(here, here, n4_s.at[zz, i], n4_r.at[zz, i], me, partner)

    def n2_start():
        for i in range(Z - 1, 0, -1):
            n2(i).start()

    def n3_start(i):
        zz = nearest(i)
        here = nbuf.at[zz, aligned(m, nq), :]
        arrived(here, n2_r.at[zz])
        for i in range(1, ys):
            n3_y(zz, i).start()
        n3_core(zz, 0).start()

    def n3_relay(zz):
        for i in range(1, ys):
            arrived(quarter(zz, m), n3_r.at[zz, i])
            n3_core(zz, i).start()

    def n3_wait(zz):
        for i in range(ys):
            arrived(quarter(zz, m), n4_r.at[zz, i])

    def turn(r):
        t3_wait(r, t3_r)
        ttr[r] = tfull[r].T

    def process(r, h):
        tile = min(256, piece_cols)

        def grad_tile(i, carry):
            at_cols = pl.ds(pl.multiple_of(h * piece_cols + i * tile, tile), tile)
            grads[r, :, at_cols] = jnp.dot(
                ttr[r], cbuf[r, h, :, aligned(i, tile)], preferred_element_type=F32
            )
            return carry

        lax.fori_loop(0, piece_cols // tile, grad_tile, 0)
        high = min(32, rows)
        sub = lax.broadcasted_iota(jnp.int32, gloc.shape, 0)
        lane = lax.broadcasted_iota(jnp.int32, gloc.shape, 1)

        def dots(g, carry):
            def row(i, sums):
                at_rows = aligned(i, high)
                at_cols = aligned(h, piece_cols)
                new = grads[r, at_rows, at_cols]
                out = []
                for q in range(group):
                    prod = new * grads[g * group + q, at_rows, at_cols]
                    terms = [
                        prod[k * 8 : k * 8 + 8, a * LANES : (a + 1) * LANES]
                        for k in range(high // 8)
                        for a in range(piece_cols // LANES)
                    ]
                    while len(terms) > 1:
                        terms = [
                            sum(terms[k + 1 : k + 2], terms[k]) for k in range(0, len(terms), 2)
                        ]
                    out.append(sums[q] + terms[0])
                return tuple(out)

            sums = lax.fori_loop(
                0, rows // high, row, tuple(jnp.zeros((8, LANES), F32) for _ in range(group))
            )
            gram = gloc[...]
            for q in range(group):
                other = g * group + q
                total = jnp.sum(jnp.sum(sums[q], axis=1, keepdims=True), axis=0, keepdims=True)
                here = ((sub == r) & (lane == other)) | ((sub == other) & (lane == r))
                gram = gram + jnp.where(here, total, 0.0)
            gloc[...] = gram
            return carry

        lax.fori_loop(0, R // group, dots, 0)

    def step(j, carry):
        zz = nearest(j)

        @pl.when((j >= 1) & (j < Z - 1))
        def _():
            pass_from(j + 1)

        pl.when((j == 1) & (Z > 2))(lambda: t3_start(2))
        pl.when((j >= 1) & (j < Z - 2))(lambda: t3_start(j + 2))
        pl.when(j == max(Z - 1, 0))(n2_start)

        @pl.when(j < Z)
        def _():
            r = at(zz, x)
            for o in range(X):
                turn(at(zz, other_x(o)))

            def one(h, inner):
                process(r, h)
                return inner

            lax.fori_loop(0, parts, one, 0)

        @pl.when(j >= 1)
        def _():
            for o in range(1, X):
                r = at(nearest(j - 1), other_x(o))

                def one(h, inner):
                    arrived(cbuf.at[r, h], c_rs.at[r, h])
                    process(r, h)
                    return inner

                lax.fori_loop(0, parts, one, 0)

        return carry

    lax.fori_loop(0, Z + 1, step, 0)

    def gm(o):
        return remote(gmp.at[m], gmp.at[m], gm_s.at[o], gm_r.at[o], me, other_m(o))

    def gr(o):
        return remote(grep.at[me], grep.at[me], gr_s.at[o], gr_r.at[o], other_r(o), m)

    gmp[m] = gloc[...]
    for o in range(1, M):
        gm(o).start()
    for i in range(Z - 1, 1, -1):
        n3_start(i)
    for o in range(1, M):
        gm(o).wait_recv()
    total = gmp[0]
    for o in range(1, M):
        total = total + gmp[o]
    grep[me] = total
    for o in range(1, R):
        gr(o).start()
    if Z > 1:
        n3_start(1)
    for o in range(1, R):
        gr(o).wait_recv()
    gram = grep[0]
    for o in range(1, R):
        gram = gram + grep[o]

    sub = lax.broadcasted_iota(jnp.int32, (grows, LANES), 0)
    lane = lax.broadcasted_iota(jnp.int32, (grows, LANES), 1)
    lane1 = lax.broadcasted_iota(jnp.int32, (1, LANES), 1)
    coef = jnp.ones((1, LANES), F32)
    count = R
    while count > 1:
        half = count // 2
        inside = (sub < count) & (lane < count)
        gram = jnp.where(inside, gram, 0.0)
        diagonal = jnp.where(sub == lane, gram, 0.0)
        crossed = jnp.where((sub == lane + half) | (lane == sub + half), gram, 0.0)
        factors = []
        for axis in (0, 1):
            square = jnp.sum(diagonal, axis=axis, keepdims=True)
            cross = jnp.sum(crossed, axis=axis, keepdims=True)
            factors.append(1.0 - cross / (2.0 * square + eps))
        scaled = jnp.where(inside, factors[0] * gram * factors[1], 0.0)
        scaled = scaled + pltpu.roll(scaled, LANES - half, 1)
        gram = scaled + pltpu.roll(scaled, grows - half, 0)
        along = jnp.broadcast_to(jnp.where(lane1 < count, factors[0], 0.0), (8, LANES))
        reach = count
        while reach < R:
            along = along + pltpu.roll(along, reach, 1)
            reach *= 2
        coef = coef * along[:1]
        count = half
    weights = [
        jnp.sum(jnp.where(lane1 == r, coef, 0.0), axis=1, keepdims=True) for r in range(R)
    ]

    own[1].wait()
    tall = min(64, rows)

    def w_rows(xx):
        return aligned(xx, rows)

    def w_across(b, o):
        piece = wbuf.at[w_rows(x), aligned(b, width)]
        return remote(piece, piece, w_s.at[b, o], w_r.at[b, x], at(z, other_x(o)), m)

    def update(b, carry):
        at_cols = aligned(b, width)

        def row(i, inner):
            at_rows = aligned(i, tall)
            total = weights[0] * grads[0, at_rows, at_cols]
            for r in range(1, R):
                total = total + weights[r] * grads[r, at_rows, at_cols]
            new = wown[at_rows, at_cols].astype(F32) - learning_rate * total
            wbuf[pl.ds(pl.multiple_of(x * rows + i * tall, tall), tall), at_cols] = new.astype(
                BF16
            )
            return inner

        lax.fori_loop(0, rows // tall, row, 0)
        for o in range(1, X):
            w_across(b, o).start()
        return carry

    lax.fori_loop(0, blocks, update, 0)
    w_out = pltpu.make_async_copy(wbuf.at[w_rows(x), :], wo_hbm, local_sem.at[3])
    w_out.start()

    def r_send(dest, b):
        to = jnp.where(dest > z, z + 1, z - 1)
        slot = jnp.where((to == dest) & (dest < z), Z, dest)
        at_cols = aligned(b, width)
        return remote(
            rsend.at[dest, :, at_cols],
            rrecv.at[slot, :, at_cols],
            rs_s.at[dest, b],
            rs_r.at[slot, b],
            at(to, x),
            m,
        )

    def r_wait(slot, b):
        piece = rrecv.at[slot, :, aligned(b, width)]
        arrived(piece, rs_r.at[slot, b])

    scale = cols * M

    def product(dest, b):
        return jnp.dot(nbuf[dest], wbuf[:, aligned(b, width)], preferred_element_type=F32)

    def pass_on(dest, b):
        at_cols = aligned(b, width)
        before = jnp.where(dest > z, z - 1, z + 1)
        more = (before >= 0) & (before < Z)
        part[...] = product(dest, b)

        @pl.when(more)
        def _():
            r_wait(dest, b)
            rsend[dest, :, at_cols] = (part[...] + rrecv[dest, :, at_cols].astype(F32)).astype(
                BF16
            )

        @pl.when(jnp.logical_not(more))
        def _():
            rsend[dest, :, at_cols] = part[...].astype(BF16)

        r_send(dest, b).start()

    def far(b, carry):
        for o in range(1, X):
            xx = other_x(o)
            arrived(wbuf.at[w_rows(xx), aligned(b, width)], w_r.at[b, xx])
        if Z > 1:
            pl.when(b == blocks // 2)(lambda: n3_relay(nearest(1)))

        def one(i, inner):
            dest = nearest(Z - 1 - i)
            wanted = jnp.abs(dest - z) >= 2
            pl.when(wanted & (b == 0))(lambda: n3_wait(dest))
            pl.when(wanted)(lambda: pass_on(dest, b))
            return inner

        return lax.fori_loop(0, Z - 1, one, carry)

    def near(b, carry):
        def one(i, inner):
            dest = nearest(Z - 1 - i)
            wanted = jnp.abs(dest - z) == 1
            pl.when(wanted & (b == 0))(lambda: n3_wait(dest))
            pl.when(wanted)(lambda: pass_on(dest, b))
            return inner

        return lax.fori_loop(0, Z - 1, one, carry)

    def stay(b, carry):
        qsum[:, aligned(b, width)] = product(z, b)
        return carry

    def finish(b, carry):
        at_cols = aligned(b, width)

        @pl.when(z > 0)
        def _():
            r_wait(z, b)
            qsum[:, at_cols] = qsum[:, at_cols] + rrecv[z, :, at_cols].astype(F32)

        @pl.when(z < Z - 1)
        def _():
            r_wait(Z, b)
            qsum[:, at_cols] = qsum[:, at_cols] + rrecv[Z, :, at_cols].astype(F32)

        qbuf[:, at_cols] = (qsum[:, at_cols] * scale**-0.5).astype(BF16)
        return carry

    for i in range(Z - 1, 1, -1):
        n3_relay(nearest(i))
    lax.fori_loop(0, blocks, far, 0)
    lax.fori_loop(0, blocks, near, 0)
    own[0].wait()
    lax.fori_loop(0, blocks, stay, 0)
    lax.fori_loop(0, blocks, finish, 0)
    q_out = pltpu.make_async_copy(qbuf, q_hbm, local_sem.at[4])
    q_out.start()

    for h in range(parts):
        pl.when(z < Z - 1)(lambda h=h: c_up(h).wait_send())
        pl.when(z > 0)(lambda h=h: c_down(h).wait_send())
        for j in range(Z):
            for o in range(1, X):
                c_across(j, h, o).wait_send()
        for j in range(1, Z):
            ok, copy = c_forward(j, h)
            pl.when(ok)(lambda copy=copy: copy().wait_send())
    for j in range(Z):
        for o in range(1 if j == 0 else 0, X):
            t2(j, o).wait_send()
    for o in range(1, M):
        gm(o).wait_send()
    for o in range(1, R):
        gr(o).wait_send()
    for o in range(1, M):
        t1(o).wait_send()
    for r in range(R):
        t3_wait(r, t3_s)
    for i in range(1, Z):
        n2(i).wait_send()
        zz = nearest(i)
        for k in range(ys):
            if k > 0:
                n3_y(zz, k).wait_send()
            n3_core(zz, k).wait_send()
    for b in range(blocks):
        for o in range(1, X):
            w_across(b, o).wait_send()
        for i in range(1, Z):
            r_send(nearest(i), b).wait_send()
    w_out.wait()
    q_out.wait()


def settle(pieces, w_in, q_in, w_out, q_out, w_held, q_held, sems):
    moves = []
    for src, held, dst, base in ((w_in, w_held, w_out, 0), (q_in, q_held, q_out, pieces)):
        tall = src.shape[0] // pieces
        for i in range(pieces):
            at_rows = pl.ds(i * tall, tall)
            moves.append(
                (
                    pltpu.make_async_copy(src.at[at_rows], held.at[at_rows], sems.at[0, base + i]),
                    pltpu.make_async_copy(held.at[at_rows], dst.at[at_rows], sems.at[1, base + i]),
                )
            )
    for get, _ in moves:
        get.start()
    for get, put in moves:
        get.wait()
        put.start()
    for _, put in moves:
        put.wait()


def local(weight, tokens, cotangent, next_tokens):
    R = lax.axis_size("rep")
    M = lax.axis_size("mp")
    X = x_size(R)
    Z = R // X
    tok, cols = cotangent.shape
    rows = weight.shape[0]
    ntok = next_tokens.shape[0]
    width = min(128, cols)
    parts = 2 if cols % (2 * LANES) == 0 else 1
    blocks = cols // width
    grows = max(8, R)
    dma = pltpu.SemaphoreType.DMA
    anywhere = pl.BlockSpec(memory_space=pl.ANY)
    results = pl.pallas_call(
        functools.partial(kernel, (Z, X, M, width)),
        out_shape=(
            jax.ShapeDtypeStruct((rows, cols), BF16),
            jax.ShapeDtypeStruct((ntok, cols), BF16),
        ),
        in_specs=[anywhere] * 4,
        out_specs=(anywhere, anywhere),
        scratch_shapes=[
            pltpu.VMEM((R, parts, tok, cols // parts), BF16),
            pltpu.VMEM((tok // M, M * cols), BF16),
            pltpu.VMEM((R, tok, rows), BF16),
            pltpu.VMEM((R, rows, tok), BF16),
            pltpu.VMEM((Z, ntok, X * rows), BF16),
            pltpu.VMEM((R, rows, cols), F32),
            pltpu.VMEM((grows, LANES), F32),
            pltpu.VMEM((M, grows, LANES), F32),
            pltpu.VMEM((R, grows, LANES), F32),
            pltpu.VMEM((rows, cols), BF16),
            pltpu.VMEM((X * rows, cols), BF16),
            pltpu.VMEM((ntok, width), F32),
            pltpu.VMEM((ntok, cols), F32),
            pltpu.VMEM((Z, ntok, cols), BF16),
            pltpu.VMEM((Z + 1, ntok, cols), BF16),
            pltpu.VMEM((ntok, cols), BF16),
            dma((5 + parts,)),
            dma((2, parts)),
            dma((Z, parts)),
            dma((Z, parts, X)),
            dma((R, parts)),
            dma((M,)),
            dma((M,)),
            dma((R,)),
            dma((R,)),
            dma((R,)),
            dma((R,)),
            dma((Z,)),
            dma((Z,)),
            dma((Z, M // 2)),
            dma((Z, M // 2)),
            dma((Z, M // 2)),
            dma((Z, M // 2)),
            dma((M,)),
            dma((M,)),
            dma((R,)),
            dma((R,)),
            dma((blocks, X)),
            dma((blocks, X)),
            dma((Z, blocks)),
            dma((Z + 1, blocks)),
        ],
        compiler_params=pltpu.CompilerParams(
            collective_id=0, has_side_effects=True, vmem_limit_bytes=60 * 1024 * 1024
        ),
    )(weight, tokens, cotangent, next_tokens)
    pieces = 4
    return pl.pallas_call(
        functools.partial(settle, pieces),
        out_shape=(
            jax.ShapeDtypeStruct((rows, cols), BF16),
            jax.ShapeDtypeStruct((ntok, cols), BF16),
        ),
        in_specs=[anywhere] * 2,
        out_specs=(anywhere, anywhere),
        scratch_shapes=[
            pltpu.VMEM((rows, cols), BF16),
            pltpu.VMEM((ntok, cols), BF16),
            dma((2, 2 * pieces)),
        ],
    )(*results)


def solution(mesh):
    in_specs = (P("rep", "mp"), P("rep", "mp"), P("rep", "mp"), P("rep", None))
    out_specs = (P("rep", "mp"), P("rep", "mp"))
    return jax.shard_map(local, mesh=mesh, in_specs=in_specs, out_specs=out_specs, check_vma=False)
```

```python
import functools

import jax
import jax.numpy as jnp
from jax import lax
from jax.experimental import pallas as pl
from jax.experimental.pallas import tpu as pltpu
from jax.sharding import PartitionSpec as P

learning_rate = 0.002
eps = 1e-06
F32 = jnp.float32
BF16 = jnp.bfloat16
MESH = pl.DeviceIdType.MESH
LANES = 128


def x_size(replicas):
    x = 1
    while 2 * (2 * x) ** 2 <= replicas and replicas % (2 * x) == 0:
        x *= 2
    return x


def aligned(start, size):
    return pl.ds(pl.multiple_of(start * size, size), size)


def kernel(
    sizes,
    w_hbm,
    t_hbm,
    c_hbm,
    n_hbm,
    wo_hbm,
    q_hbm,
    cbuf,
    t1buf,
    tfull,
    ttr,
    nbuf,
    grads,
    gloc,
    gmp,
    grep,
    wown,
    wbuf,
    part,
    qsum,
    rsend,
    rrecv,
    qbuf,
    local_sem,
    c_own,
    c_fwd,
    c_xs,
    c_rs,
    t1_s,
    t1_r,
    t2_s,
    t2_r,
    t3_s,
    t3_r,
    n2_s,
    n2_r,
    n3_s,
    n3_r,
    n4_s,
    n4_r,
    gm_s,
    gm_r,
    gr_s,
    gr_r,
    w_s,
    w_r,
    rs_s,
    rs_r,
):
    Z, X, M, width = sizes
    R = Z * X
    _, parts, tok, piece_cols = cbuf.shape
    cols = parts * piece_cols
    rows = tfull.shape[2]
    feats = X * rows
    tq = tok // M
    ntok = nbuf.shape[1]
    nq = ntok // M
    blocks = cols // width
    group = min(8, R)
    grows = gloc.shape[0]

    me = lax.axis_index("rep")
    m = lax.axis_index("mp")
    z = me // X
    x = lax.rem(me, X)

    def nearest(j):
        found = jnp.int32(0)
        for a in range(Z):
            order = sorted(range(Z), key=lambda b: (abs(b - a), b))
            for i in range(Z):
                found = found + jnp.where((z == a) & (j == i), order[i], 0)
        return found

    def remote(src, dst, send, recv, r, mm):
        return pltpu.make_async_remote_copy(
            src_ref=src,
            dst_ref=dst,
            send_sem=send,
            recv_sem=recv,
            device_id=(r, mm),
            device_id_type=MESH,
        )

    def arrived(piece, sem):
        pltpu.make_async_copy(piece, piece, sem).wait()

    def other_x(o):
        return lax.rem(x + o, X)

    def other_m(o):
        return lax.rem(m + o, M)

    ys = M // 2
    y = m // 2
    core = lax.rem(m, 2)
    partner = y * 2 + 1 - core

    def other_y(i):
        return lax.rem(y + i, ys) * 2 + core

    def from_y(i):
        return lax.rem(y + ys - i, ys) * 2 + core

    def other_r(o):
        return lax.rem(me + o, R)

    def at(zz, xx):
        return zz * X + xx

    def c_mine(h):
        return c_hbm.at[:, aligned(h, piece_cols)]

    def own_copies():
        copies = [
            pltpu.make_async_copy(c_mine(h), cbuf.at[me, h], local_sem.at[5 + h])
            for h in range(parts)
        ]
        own_tokens = t1buf.at[:, aligned(m, cols)]
        return [
            pltpu.make_async_copy(n_hbm.at[:, aligned(z, feats)], nbuf.at[z], local_sem.at[0]),
            pltpu.make_async_copy(w_hbm, wown, local_sem.at[1]),
            pltpu.make_async_copy(t_hbm.at[aligned(m, tq), :], own_tokens, local_sem.at[2]),
        ] + copies

    for copy in own_copies():
        copy.start()

    barrier = pltpu.get_barrier_semaphore()
    for o in range(1, M):
        pl.semaphore_signal(barrier, inc=1, device_id=(me, other_m(o)), device_id_type=MESH)
    for o in range(1, R):
        pl.semaphore_signal(barrier, inc=1, device_id=(other_r(o), m), device_id_type=MESH)
    pl.semaphore_wait(barrier, M + R - 2)

    def t1(o):
        mm = other_m(o)
        return remote(
            t_hbm.at[aligned(mm, tq), :],
            t1buf.at[:, aligned(m, cols)],
            t1_s.at[o],
            t1_r.at[o],
            me,
            mm,
        )

    for o in range(1, M):
        t1(o).start()

    def c_up(h):
        return remote(
            c_mine(h), cbuf.at[me, h], c_own.at[0, h], c_rs.at[me, h], at(z + 1, x), m
        )

    def c_down(h):
        return remote(
            c_mine(h), cbuf.at[me, h], c_own.at[1, h], c_rs.at[me, h], at(z - 1, x), m
        )

    def c_across(j, h, o):
        r = at(nearest(j), x)
        here = cbuf.at[r, h]
        return remote(here, here, c_xs.at[j, h, o], c_rs.at[r, h], at(z, other_x(o)), m)

    def c_forward(j, h):
        zz = nearest(j)
        r = at(zz, x)
        to = jnp.where(zz < z, z + 1, z - 1)
        here = cbuf.at[r, h]
        return (
            (to >= 0) & (to < Z),
            lambda: remote(here, here, c_fwd.at[j, h], c_rs.at[r, h], at(to, x), m),
        )

    own = own_copies()
    for h in range(parts):
        pl.when(z < Z - 1)(lambda h=h: c_up(h).start())
        pl.when(z > 0)(lambda h=h: c_down(h).start())
        own[3 + h].wait()
        for o in range(1, X):
            c_across(0, h, o).start()

    def zero(i, carry):
        for r in range(R):
            grads[r, aligned(i, 8), :] = jnp.zeros((8, cols), F32)
        return carry

    lax.fori_loop(0, rows // 8, zero, 0)
    gloc[...] = jnp.zeros_like(gloc)

    own[2].wait()
    for o in range(1, M):
        t1(o).wait_recv()

    def t2(j, o):
        r = at(nearest(j), other_x(o))
        return remote(
            t1buf.at[:, aligned(r, rows)],
            tfull.at[me, aligned(m, tq), :],
            t2_s.at[j * X + o],
            t2_r.at[me],
            r,
            m,
        )

    mine = tfull.at[me, aligned(m, tq), :]
    pltpu.make_async_copy(t1buf.at[:, aligned(me, rows)], mine, t2_r.at[me]).start()
    for j in range(Z):
        for o in range(1 if j == 0 else 0, X):
            t2(j, o).start()

    def t3(r, o):
        here = tfull.at[r, aligned(m, tq), :]
        return remote(here, here, t3_s.at[r], t3_r.at[r], me, other_m(o))

    def t3_start(j):
        for xo in range(X):
            r = at(nearest(j), other_x(xo))
            arrived(tfull.at[r, aligned(m, tq), :], t2_r.at[r])
            for o in range(1, M):
                t3(r, o).start()

    def t3_wait(r, sem):
        arrived(tfull.at[r, pl.ds(0, (M - 1) * tq), :], sem.at[r])

    def pass_cotangent(j):
        r = at(nearest(j), x)
        for h in range(parts):
            arrived(cbuf.at[r, h], c_rs.at[r, h])
            ok, copy = c_forward(j, h)
            pl.when(ok)(lambda copy=copy: copy().start())
            for o in range(1, X):
                c_across(j, h, o).start()

    def pass_from(distance):
        def one(j, carry):
            pl.when(jnp.abs(nearest(j) - z) == distance)(lambda: pass_cotangent(j))
            return carry

        lax.fori_loop(1, Z, one, 0)

    pass_from(1)
    for j in range(min(2, Z)):
        t3_start(j)

    def n2(i):
        zz = nearest(i)
        return remote(
            n_hbm.at[aligned(m, nq), aligned(zz, feats)],
            nbuf.at[z, aligned(m, nq), :],
            n2_s.at[i],
            n2_r.at[z],
            at(zz, x),
            m,
        )

    def quarter(zz, q):
        return nbuf.at[zz, aligned(q, nq), :]

    def n3_y(zz, i):
        here = quarter(zz, m)
        return remote(here, here, n3_s.at[zz, i], n3_r.at[zz, i], me, other_y(i))

    def n3_core(zz, i):
        here = quarter(zz, m if i == 0 else from_y(i))
        return remote(here, here, n4_s.at[zz, i], n4_r.at[zz, i], me, partner)

    def n2_start():
        for i in range(Z - 1, 0, -1):
            n2(i).start()

    def n3_start(i):
        zz = nearest(i)
        here = nbuf.at[zz, aligned(m, nq), :]
        arrived(here, n2_r.at[zz])
        for i in range(1, ys):
            n3_y(zz, i).start()
        n3_core(zz, 0).start()

    def n3_relay(zz):
        for i in range(1, ys):
            arrived(quarter(zz, m), n3_r.at[zz, i])
            n3_core(zz, i).start()

    def n3_wait(zz):
        for i in range(ys):
            arrived(quarter(zz, m), n4_r.at[zz, i])

    def turn(r):
        t3_wait(r, t3_r)
        ttr[r] = tfull[r].T

    def process(r, h):
        tile = min(256, piece_cols)

        def grad_tile(i, carry):
            at_cols = pl.ds(pl.multiple_of(h * piece_cols + i * tile, tile), tile)
            grads[r, :, at_cols] = jnp.dot(
                ttr[r], cbuf[r, h, :, aligned(i, tile)], preferred_element_type=F32
            )
            return carry

        lax.fori_loop(0, piece_cols // tile, grad_tile, 0)
        high = min(32, rows)
        sub = lax.broadcasted_iota(jnp.int32, gloc.shape, 0)
        lane = lax.broadcasted_iota(jnp.int32, gloc.shape, 1)

        def dots(g, carry):
            def row(i, sums):
                at_rows = aligned(i, high)
                at_cols = aligned(h, piece_cols)
                new = grads[r, at_rows, at_cols]
                out = []
                for q in range(group):
                    prod = new * grads[g * group + q, at_rows, at_cols]
                    terms = [
                        prod[k * 8 : k * 8 + 8, a * LANES : (a + 1) * LANES]
                        for k in range(high // 8)
                        for a in range(piece_cols // LANES)
                    ]
                    while len(terms) > 1:
                        terms = [
                            sum(terms[k + 1 : k + 2], terms[k]) for k in range(0, len(terms), 2)
                        ]
                    out.append(sums[q] + terms[0])
                return tuple(out)

            sums = lax.fori_loop(
                0, rows // high, row, tuple(jnp.zeros((8, LANES), F32) for _ in range(group))
            )
            gram = gloc[...]
            for q in range(group):
                other = g * group + q
                total = jnp.sum(jnp.sum(sums[q], axis=1, keepdims=True), axis=0, keepdims=True)
                here = ((sub == r) & (lane == other)) | ((sub == other) & (lane == r))
                gram = gram + jnp.where(here, total, 0.0)
            gloc[...] = gram
            return carry

        lax.fori_loop(0, R // group, dots, 0)

    def step(j, carry):
        zz = nearest(j)

        @pl.when((j >= 1) & (j < Z - 1))
        def _():
            pass_from(j + 1)

        pl.when((j == 1) & (Z > 2))(lambda: t3_start(2))
        pl.when((j >= 1) & (j < Z - 2))(lambda: t3_start(j + 2))
        pl.when(j == max(Z - 1, 0))(n2_start)

        @pl.when(j >= 1)
        def _():
            for o in range(1, X):
                r = at(nearest(j - 1), other_x(o))

                def one(h, inner):
                    arrived(cbuf.at[r, h], c_rs.at[r, h])
                    process(r, h)
                    return inner

                lax.fori_loop(0, parts, one, 0)

        @pl.when(j < Z)
        def _():
            r = at(zz, x)
            for o in range(X):
                turn(at(zz, other_x(o)))

            def one(h, inner):
                process(r, h)
                return inner

            lax.fori_loop(0, parts, one, 0)

        return carry

    lax.fori_loop(0, Z + 1, step, 0)

    def gm(o):
        return remote(gmp.at[m], gmp.at[m], gm_s.at[o], gm_r.at[o], me, other_m(o))

    def gr(o):
        return remote(grep.at[me], grep.at[me], gr_s.at[o], gr_r.at[o], other_r(o), m)

    gmp[m] = gloc[...]
    for o in range(1, M):
        gm(o).start()
    for i in range(Z - 1, 1, -1):
        n3_start(i)
    for o in range(1, M):
        gm(o).wait_recv()
    total = gmp[0]
    for o in range(1, M):
        total = total + gmp[o]
    grep[me] = total
    for o in range(1, R):
        gr(o).start()
    if Z > 1:
        n3_start(1)
    for o in range(1, R):
        gr(o).wait_recv()
    gram = grep[0]
    for o in range(1, R):
        gram = gram + grep[o]

    sub = lax.broadcasted_iota(jnp.int32, (grows, LANES), 0)
    lane = lax.broadcasted_iota(jnp.int32, (grows, LANES), 1)
    lane1 = lax.broadcasted_iota(jnp.int32, (1, LANES), 1)
    coef = jnp.ones((1, LANES), F32)
    count = R
    while count > 1:
        half = count // 2
        inside = (sub < count) & (lane < count)
        gram = jnp.where(inside, gram, 0.0)
        diagonal = jnp.where(sub == lane, gram, 0.0)
        crossed = jnp.where((sub == lane + half) | (lane == sub + half), gram, 0.0)
        factors = []
        for axis in (0, 1):
            square = jnp.sum(diagonal, axis=axis, keepdims=True)
            cross = jnp.sum(crossed, axis=axis, keepdims=True)
            factors.append(1.0 - cross / (2.0 * square + eps))
        scaled = jnp.where(inside, factors[0] * gram * factors[1], 0.0)
        scaled = scaled + pltpu.roll(scaled, LANES - half, 1)
        gram = scaled + pltpu.roll(scaled, grows - half, 0)
        along = jnp.broadcast_to(jnp.where(lane1 < count, factors[0], 0.0), (8, LANES))
        reach = count
        while reach < R:
            along = along + pltpu.roll(along, reach, 1)
            reach *= 2
        coef = coef * along[:1]
        count = half
    weights = [
        jnp.sum(jnp.where(lane1 == r, coef, 0.0), axis=1, keepdims=True) for r in range(R)
    ]

    own[1].wait()
    tall = min(64, rows)

    def w_rows(xx):
        return aligned(xx, rows)

    def w_across(b, o):
        piece = wbuf.at[w_rows(x), aligned(b, width)]
        return remote(piece, piece, w_s.at[b, o], w_r.at[b, x], at(z, other_x(o)), m)

    def update(b, carry):
        at_cols = aligned(b, width)

        def row(i, inner):
            at_rows = aligned(i, tall)
            total = weights[0] * grads[0, at_rows, at_cols]
            for r in range(1, R):
                total = total + weights[r] * grads[r, at_rows, at_cols]
            new = wown[at_rows, at_cols].astype(F32) - learning_rate * total
            wbuf[pl.ds(pl.multiple_of(x * rows + i * tall, tall), tall), at_cols] = new.astype(
                BF16
            )
            return inner

        lax.fori_loop(0, rows // tall, row, 0)
        for o in range(1, X):
            w_across(b, o).start()
        return carry

    lax.fori_loop(0, blocks, update, 0)
    w_out = pltpu.make_async_copy(wbuf.at[w_rows(x), :], wo_hbm, local_sem.at[3])
    w_out.start()

    def r_send(dest, b):
        to = jnp.where(dest > z, z + 1, z - 1)
        slot = jnp.where((to == dest) & (dest < z), Z, dest)
        at_cols = aligned(b, width)
        return remote(
            rsend.at[dest, :, at_cols],
            rrecv.at[slot, :, at_cols],
            rs_s.at[dest, b],
            rs_r.at[slot, b],
            at(to, x),
            m,
        )

    def r_wait(slot, b):
        piece = rrecv.at[slot, :, aligned(b, width)]
        arrived(piece, rs_r.at[slot, b])

    scale = cols * M

    def product(dest, b):
        return jnp.dot(nbuf[dest], wbuf[:, aligned(b, width)], preferred_element_type=F32)

    def pass_on(dest, b):
        at_cols = aligned(b, width)
        before = jnp.where(dest > z, z - 1, z + 1)
        more = (before >= 0) & (before < Z)
        part[...] = product(dest, b)

        @pl.when(more)
        def _():
            r_wait(dest, b)
            rsend[dest, :, at_cols] = (part[...] + rrecv[dest, :, at_cols].astype(F32)).astype(
                BF16
            )

        @pl.when(jnp.logical_not(more))
        def _():
            rsend[dest, :, at_cols] = part[...].astype(BF16)

        r_send(dest, b).start()

    def far(b, carry):
        for o in range(1, X):
            xx = other_x(o)
            arrived(wbuf.at[w_rows(xx), aligned(b, width)], w_r.at[b, xx])
        if Z > 1:
            pl.when(b == blocks // 2)(lambda: n3_relay(nearest(1)))

        def one(i, inner):
            dest = nearest(Z - 1 - i)
            wanted = jnp.abs(dest - z) >= 2
            pl.when(wanted & (b == 0))(lambda: n3_wait(dest))
            pl.when(wanted)(lambda: pass_on(dest, b))
            return inner

        return lax.fori_loop(0, Z - 1, one, carry)

    def near(b, carry):
        def one(i, inner):
            dest = nearest(Z - 1 - i)
            wanted = jnp.abs(dest - z) == 1
            pl.when(wanted & (b == 0))(lambda: n3_wait(dest))
            pl.when(wanted)(lambda: pass_on(dest, b))
            return inner

        return lax.fori_loop(0, Z - 1, one, carry)

    def stay(b, carry):
        qsum[:, aligned(b, width)] = product(z, b)
        return carry

    def finish(b, carry):
        at_cols = aligned(b, width)

        @pl.when(z > 0)
        def _():
            r_wait(z, b)
            qsum[:, at_cols] = qsum[:, at_cols] + rrecv[z, :, at_cols].astype(F32)

        @pl.when(z < Z - 1)
        def _():
            r_wait(Z, b)
            qsum[:, at_cols] = qsum[:, at_cols] + rrecv[Z, :, at_cols].astype(F32)

        qbuf[:, at_cols] = (qsum[:, at_cols] * scale**-0.5).astype(BF16)
        return carry

    for i in range(Z - 1, 1, -1):
        n3_relay(nearest(i))
    lax.fori_loop(0, blocks, far, 0)
    lax.fori_loop(0, blocks, near, 0)
    own[0].wait()
    lax.fori_loop(0, blocks, stay, 0)
    lax.fori_loop(0, blocks, finish, 0)
    q_out = pltpu.make_async_copy(qbuf, q_hbm, local_sem.at[4])
    q_out.start()

    for h in range(parts):
        pl.when(z < Z - 1)(lambda h=h: c_up(h).wait_send())
        pl.when(z > 0)(lambda h=h: c_down(h).wait_send())
        for j in range(Z):
            for o in range(1, X):
                c_across(j, h, o).wait_send()
        for j in range(1, Z):
            ok, copy = c_forward(j, h)
            pl.when(ok)(lambda copy=copy: copy().wait_send())
    for j in range(Z):
        for o in range(1 if j == 0 else 0, X):
            t2(j, o).wait_send()
    for o in range(1, M):
        gm(o).wait_send()
    for o in range(1, R):
        gr(o).wait_send()
    for o in range(1, M):
        t1(o).wait_send()
    for r in range(R):
        t3_wait(r, t3_s)
    for i in range(1, Z):
        n2(i).wait_send()
        zz = nearest(i)
        for k in range(ys):
            if k > 0:
                n3_y(zz, k).wait_send()
            n3_core(zz, k).wait_send()
    for b in range(blocks):
        for o in range(1, X):
            w_across(b, o).wait_send()
        for i in range(1, Z):
            r_send(nearest(i), b).wait_send()
    w_out.wait()
    q_out.wait()


def settle(pieces, w_in, q_in, w_out, q_out, w_held, q_held, sems):
    moves = []
    for src, held, dst, base in ((w_in, w_held, w_out, 0), (q_in, q_held, q_out, pieces)):
        tall = src.shape[0] // pieces
        for i in range(pieces):
            at_rows = pl.ds(i * tall, tall)
            moves.append(
                (
                    pltpu.make_async_copy(src.at[at_rows], held.at[at_rows], sems.at[0, base + i]),
                    pltpu.make_async_copy(held.at[at_rows], dst.at[at_rows], sems.at[1, base + i]),
                )
            )
    for get, _ in moves:
        get.start()
    for get, put in moves:
        get.wait()
        put.start()
    for _, put in moves:
        put.wait()


def local(weight, tokens, cotangent, next_tokens):
    R = lax.axis_size("rep")
    M = lax.axis_size("mp")
    X = x_size(R)
    Z = R // X
    tok, cols = cotangent.shape
    rows = weight.shape[0]
    ntok = next_tokens.shape[0]
    width = min(128, cols)
    parts = 2 if cols % (2 * LANES) == 0 else 1
    blocks = cols // width
    grows = max(8, R)
    dma = pltpu.SemaphoreType.DMA
    anywhere = pl.BlockSpec(memory_space=pl.ANY)
    results = pl.pallas_call(
        functools.partial(kernel, (Z, X, M, width)),
        out_shape=(
            jax.ShapeDtypeStruct((rows, cols), BF16),
            jax.ShapeDtypeStruct((ntok, cols), BF16),
        ),
        in_specs=[anywhere] * 4,
        out_specs=(anywhere, anywhere),
        scratch_shapes=[
            pltpu.VMEM((R, parts, tok, cols // parts), BF16),
            pltpu.VMEM((tok // M, M * cols), BF16),
            pltpu.VMEM((R, tok, rows), BF16),
            pltpu.VMEM((R, rows, tok), BF16),
            pltpu.VMEM((Z, ntok, X * rows), BF16),
            pltpu.VMEM((R, rows, cols), F32),
            pltpu.VMEM((grows, LANES), F32),
            pltpu.VMEM((M, grows, LANES), F32),
            pltpu.VMEM((R, grows, LANES), F32),
            pltpu.VMEM((rows, cols), BF16),
            pltpu.VMEM((X * rows, cols), BF16),
            pltpu.VMEM((ntok, width), F32),
            pltpu.VMEM((ntok, cols), F32),
            pltpu.VMEM((Z, ntok, cols), BF16),
            pltpu.VMEM((Z + 1, ntok, cols), BF16),
            pltpu.VMEM((ntok, cols), BF16),
            dma((5 + parts,)),
            dma((2, parts)),
            dma((Z, parts)),
            dma((Z, parts, X)),
            dma((R, parts)),
            dma((M,)),
            dma((M,)),
            dma((R,)),
            dma((R,)),
            dma((R,)),
            dma((R,)),
            dma((Z,)),
            dma((Z,)),
            dma((Z, M // 2)),
            dma((Z, M // 2)),
            dma((Z, M // 2)),
            dma((Z, M // 2)),
            dma((M,)),
            dma((M,)),
            dma((R,)),
            dma((R,)),
            dma((blocks, X)),
            dma((blocks, X)),
            dma((Z, blocks)),
            dma((Z + 1, blocks)),
        ],
        compiler_params=pltpu.CompilerParams(
            collective_id=0, has_side_effects=True, vmem_limit_bytes=60 * 1024 * 1024
        ),
    )(weight, tokens, cotangent, next_tokens)
    pieces = 4
    return pl.pallas_call(
        functools.partial(settle, pieces),
        out_shape=(
            jax.ShapeDtypeStruct((rows, cols), BF16),
            jax.ShapeDtypeStruct((ntok, cols), BF16),
        ),
        in_specs=[anywhere] * 2,
        out_specs=(anywhere, anywhere),
        scratch_shapes=[
            pltpu.VMEM((rows, cols), BF16),
            pltpu.VMEM((ntok, cols), BF16),
            dma((2, 2 * pieces)),
        ],
    )(*results)


def solution(mesh):
    in_specs = (P("rep", "mp"), P("rep", "mp"), P("rep", "mp"), P("rep", None))
    out_specs = (P("rep", "mp"), P("rep", "mp"))
    return jax.shard_map(local, mesh=mesh, in_specs=in_specs, out_specs=out_specs, check_vma=False)
```
